512 devices in a mesh: dom: 64 (over x, y, z_lo), col: 8 (over z_hi, core).
Axes of the slice: x: 4, y: 8, z: 8 (z_hi: 4, z_lo: 2; z = z_hi * 2 + z_lo), core: 2. Of those that a mesh axis runs over, the one named last changes fastest.
Arguments:
- inverse: bfloat16 [64, 1664, 1664], P('dom', 'col'), may hold values from -1 to 4, as said below
- trace_map: bfloat16 [64, 512, 1664], P('dom', 'col'), may hold values from -0.15625 to 0.15625
- panel_coupling: bfloat16 [64, 1664, 128], P('dom'), may hold values from -6 to 6
- coupling: float32 [64, 6, 1664], P('dom', None, 'col'), may hold values from 0.15 to 0.9
- neighbours: int32 [64, 6], P('dom'), may hold values from 0 to 63, as said below
- iface_count: int32 [64], replicated, may hold values from 26 to 104, as said below
- surface_rows: int32 [64, 8, 1, 64], P('dom', 'col'), may hold values from 0 to 63
- factor: float32 [32768, 2048], P(('dom', 'col')), may hold values from -2 to 2
- colloc: float32 [3, 32768], P(None, ('dom', 'col')), may hold values from -1 to 1
- quad_points: float32 [3, 4, 32768], P(None, None, ('dom', 'col')), may hold values from -1 to 1
- quad_weight: float32 [4, 32768], P(None, ('dom', 'col')), may hold values from 2 to 16
- panel_block: int32 [2], replicated, may hold values from 0 to 511
Outputs:
- panel_columns: float32 [32768, 128], P(('dom', 'col'))
The draws below stay inside these ranges and needn't reach their ends.
Inputs may be any that keep to these rules, and one draw needn't show every extreme that they name: Each domain's inverse is symmetric. `neighbours`: each domain lists 6 different domains, never itself. `iface_count`: some domain has exactly 104.
All inputs are finite; a program needn't handle non-finite values.
Results may differ from the reference program's by a relative error of at most 0.007.
Values may be sent and summed in bfloat16 or wider, within the bound.
No kernel may reach another device: no remote copies, remote signals or barrier semaphores. Data moves between devices by JAX's collectives and lax.ppermute only.
A program may use at most 64 MiB of HBM per device.

```python
import math
import jax
import jax.numpy as jnp
from jax import lax

M = 1664
MB = 208
IFM = 104
NB = 6
P_SIZE = 64
NPAN = 2
KPRIOR = 2048
QP = 4
ROWS = 64
SLOTS = 1
DOMAINS = 64
LANES = 8
SURF = 32768
SURF_DOF = 512


def draw_inverse(key, part):

    def domain_draw(number):
        subkey = jax.random.fold_in(key, number)
        key_one, key_two = jax.random.split(subkey, 2)
        random_part = jax.random.truncated_normal(key_one, -4.0, 4.0, (M, M), jnp.float32) * (0.5 / math.sqrt(M))
        symmetric = (random_part + random_part.T) * 0.7071
        diagonal = jax.random.uniform(key_two, (M,), jnp.float32, 0.8, 1.6)
        matrix = symmetric + jnp.diag(diagonal)
        return matrix.astype(jnp.bfloat16)
    return lax.map(domain_draw, jnp.arange(DOMAINS, dtype=jnp.int32))


def draw_neighbours(key, part):
    scores = jax.random.randint(key, (DOMAINS, DOMAINS), 0, 1 << 20) * DOMAINS + jnp.arange(DOMAINS, dtype=jnp.int32)[None, :]
    scores = jnp.where(jnp.eye(DOMAINS, dtype=jnp.bool_), jnp.int32(1 << 30), scores)
    ordering = jnp.argsort(scores, axis=1, stable=True)
    return ordering[:, :NB].astype(jnp.int32)


def draw_iface_count(key, part):
    key_one, key_two = jax.random.split(key)
    counts = jax.random.randint(key_one, (DOMAINS,), IFM // 4, IFM + 1)
    chosen = jax.random.randint(key_two, (), 0, DOMAINS)
    return counts.at[chosen].set(IFM).astype(jnp.int32)


def plant(values, stream_key, least, high):
    extent = values.shape
    index_at = [jax.random.randint(jax.random.fold_in(stream_key, axis), (), 0, extent[axis]) for axis in range(len(extent))]
    values = values.at[tuple(index_at)].set(least)
    longest = extent.index(max(extent))
    index_at[longest] = (index_at[longest] + 1) % extent[longest]
    return values.at[tuple(index_at)].set(high)


def block_scale(key, shape, cuts, least, top_value):
    loudness = 1.0
    for position, shards_of in cuts:
        heights = jax.random.uniform(jax.random.fold_in(jax.random.fold_in(key, 6), position), (shards_of,), jnp.float32, least / len(cuts), top_value / len(cuts))
        loudness = loudness * jnp.repeat(jnp.exp(heights), shape[position] // shards_of).reshape((-1,) + (1,) * (len(shape) - 1 - position))
    return loudness


def gaussian(own_key, dims, spread, bound, cuts=(), kind=jnp.bfloat16):
    array = spread * jax.random.normal(own_key, dims, jnp.float32)
    if cuts:
        array = array * block_scale(own_key, dims, cuts, -0.22, 0.18)
    return jnp.clip(array, -bound, bound).astype(kind)


def setup_inputs(seed: int = 0) -> dict:
    splits = jax.random.split(jax.random.key(seed), 13)
    inverse = draw_inverse(jax.random.fold_in(splits[12], 71), 0)
    trace_map = gaussian(splits[1], (DOMAINS, SURF_DOF, M), M ** -0.5, 0.15625, ((0, 64), (1, 8)))
    panel_coupling = gaussian(splits[2], (DOMAINS, M, NPAN * P_SIZE), 1.0, 6.0, ((0, 64),))
    coupling = jnp.clip(jnp.exp(math.log(0.9) - 1.7917594 * jax.random.uniform(splits[3], (DOMAINS, NB, M), jnp.float32) ** block_scale(splits[3], (DOMAINS, NB, M), ((0, 64), (2, 8)), -0.2, 0.2)), 0.15, 0.9)
    neighbours = draw_neighbours(jax.random.fold_in(splits[12], 71), 0)
    iface_count = draw_iface_count(jax.random.fold_in(splits[12], 71), 0)
    surface_rows = plant(jax.random.randint(splits[6], (DOMAINS, LANES, SLOTS, DOMAINS), 0, ROWS), jax.random.fold_in(splits[6], 1), 0, ROWS - 1).astype(jnp.int32)
    factor = gaussian(splits[7], (SURF, KPRIOR), (KPRIOR ** -0.25), 2.0, ((0, 512),), jnp.float32)
    colloc = jnp.clip(jax.random.uniform(splits[8], (3, SURF), jnp.float32, -1.0, 1.0) * block_scale(splits[8], (3, SURF), ((1, 512),), -0.4, 0.0), -1.0, 1.0)
    quad_points = jnp.clip(jax.random.uniform(splits[9], (3, QP, SURF), jnp.float32, -1.0, 1.0) * block_scale(splits[9], (3, QP, SURF), ((2, 512),), -0.4, 0.0), -1.0, 1.0)
    quad_weight = jnp.clip(jnp.exp(math.log(16.0) - 2.0794415 * jax.random.uniform(splits[10], (QP, SURF), jnp.float32) ** block_scale(splits[10], (QP, SURF), ((1, 512),), -0.2, 0.2)), 2.0, 16.0)
    panel_block = jax.random.randint(splits[11], (NPAN,), 0, SURF // P_SIZE).astype(jnp.int32)
    return {"inverse": inverse, "trace_map": trace_map, "panel_coupling": panel_coupling, "coupling": coupling, "neighbours": neighbours, "iface_count": iface_count, "surface_rows": surface_rows, "factor": factor, "colloc": colloc, "quad_points": quad_points, "quad_weight": quad_weight, "panel_block": panel_block}


WAVE_NUMBER = 8.0
SMOOTHING = 0.05

def kernel_rows(row_points, panel_points, panel_weights):
    shifted = row_points[:, :, None, None] - panel_points[:, None, :, :]
    squared = lax.optimization_barrier(jnp.sum(shifted * shifted, axis=0))
    green_values = jnp.cos(WAVE_NUMBER * jnp.sqrt(squared)) / (4.0 * math.pi * jnp.sqrt(squared + SMOOTHING * SMOOTHING))
    return lax.optimization_barrier(jnp.sum(panel_weights[None, :, :] * green_values, axis=1))

def reference(inverse, trace_map, panel_coupling, coupling, neighbours, iface_count, surface_rows, factor, colloc, quad_points, quad_weight, panel_block):
    column_count = NPAN * P_SIZE
    patch_rows = jnp.arange(M, dtype=jnp.int32) % MB
    live = (patch_rows[None, :] < iface_count[:, None].astype(jnp.int32)).astype(jnp.float32)

    def first_domain(inputs):
        matrix, panel_loads, live_row = inputs
        applied = jnp.dot(matrix, panel_loads, preferred_element_type=jnp.float32)
        return (applied * live_row[:, None]).astype(jnp.bfloat16)
    first_values = lax.map(first_domain, (inverse, panel_coupling, live))

    def second_domain(inputs):
        matrix, panel_loads, live_row, weights_row, listed, map_rows = inputs
        gathered = first_values[listed.astype(jnp.int32)].astype(jnp.float32)
        correction = lax.optimization_barrier(jnp.sum(weights_row[:, :, None] * gathered, axis=0))
        loaded = (panel_loads.astype(jnp.float32) - live_row[:, None] * correction).astype(jnp.bfloat16)
        second = jnp.dot(matrix, loaded, preferred_element_type=jnp.float32).astype(jnp.bfloat16)
        return jnp.dot(map_rows, second, preferred_element_type=jnp.float32).astype(jnp.bfloat16)
    traces = lax.map(second_domain, (inverse, panel_coupling, live, coupling, neighbours, trace_map))
    owner_ids = jnp.arange(DOMAINS, dtype=jnp.int32)[None, None, None, :]
    lane_ids = jnp.arange(LANES, dtype=jnp.int32)[None, :, None, None]
    local_rows = jnp.transpose(surface_rows.astype(jnp.int32), (3, 1, 2, 0))
    target_rows = ((owner_ids * LANES + lane_ids) * ROWS + local_rows).reshape(-1)
    surface_sum = jax.ops.segment_sum(traces.reshape(-1, column_count).astype(jnp.float32), target_rows, num_segments=SURF)
    factor_list = []
    points_list = []
    weights_list = []
    for panel_number in range(NPAN):
        begin_row = (panel_block[panel_number] * P_SIZE).astype(jnp.int32)
        factor_list.append(lax.dynamic_slice_in_dim(factor, begin_row, P_SIZE, 0))
        points_list.append(lax.dynamic_slice_in_dim(quad_points, begin_row, P_SIZE, 2))
        weights_list.append(lax.dynamic_slice_in_dim(quad_weight, begin_row, P_SIZE, 1))
    panel_factor = jnp.concatenate(factor_list, axis=0)
    panel_points = jnp.concatenate(points_list, axis=2)
    panel_weights = jnp.concatenate(weights_list, axis=1)

    def kernel_block(row_points):
        return kernel_rows(row_points, panel_points, panel_weights)
    blocks = jnp.transpose(colloc.reshape(3, SURF // ROWS, ROWS), (1, 0, 2))
    kernel = lax.map(kernel_block, blocks).reshape(SURF, column_count)
    prior_update = lax.dot_general(factor, panel_factor, (((1,), (1,)), ((), ())), precision=lax.Precision.HIGHEST, preferred_element_type=jnp.float32)
    return kernel - surface_sum - prior_update
```

```python
import math

import jax
import jax.numpy as jnp
from jax import lax
from jax.sharding import PartitionSpec as P

MB = 208
P_SIZE = 64
NPAN = 2
LIVE = 128
PAIR = 2
LANE = 128

WAVE_NUMBER = 8.0
SMOOTHING = 0.05

F32 = jnp.float32
BF16 = jnp.bfloat16


def split3(values):
    high = lax.reduce_precision(values, 8, 7)
    rest = values - high
    middle = lax.reduce_precision(rest, 8, 7)
    low = rest - middle
    return jnp.concatenate(
        [high.astype(BF16), middle.astype(BF16), low.astype(BF16)], axis=-1
    )


def join3(parts):
    parts = parts.astype(F32)
    width = parts.shape[-1] // 3
    return (parts[..., 2 * width :] + parts[..., width : 2 * width]) + parts[..., :width]


def local(
    inverse,
    trace_map,
    panel_coupling,
    coupling,
    neighbours,
    iface_count,
    surface_rows,
    factor,
    colloc,
    quad_points,
    quad_weight,
    panel_block,
):
    dom_index = lax.axis_index("dom")
    doms = lax.axis_size("dom")
    cols = lax.axis_size("col")
    inverse_rows = inverse[0]
    panel_loads = panel_coupling[0]
    own_count = iface_count[dom_index]
    live = (jnp.arange(LIVE, dtype=jnp.int32) < own_count).astype(F32)[:, None]

    first_apply = jnp.dot(inverse_rows[:LIVE], panel_loads, preferred_element_type=F32)
    first_values = (first_apply * live).astype(BF16).reshape(doms, PAIR, LANE)
    factor_low = factor.astype(BF16)
    chunks = factor_low.reshape(4, 16, 16, LANE).transpose(0, 2, 1, 3).reshape(doms, 16, LANE)
    quads = jnp.concatenate([quad_points.reshape(12, P_SIZE), quad_weight], axis=0).T
    weights = coupling[0][:, :LIVE].reshape(6, doms, PAIR).transpose(1, 0, 2).reshape(doms, 12)
    listed = jnp.broadcast_to(neighbours.astype(F32).astype(BF16), (doms, 6))
    misc = jnp.concatenate(
        [split3(quads), split3(weights), listed, jnp.zeros((doms, LANE - 90), BF16)], axis=1
    )
    sent = jnp.concatenate(
        [chunks, first_values, misc[:, None], jnp.zeros((doms, 5, LANE), BF16)], axis=1
    )
    got = lax.all_to_all(sent, "dom", 0, 0, tiled=True)

    misc = got[:, 18]
    weights = join3(misc[:, 48:84])
    listed = misc[:, 84:90].astype(F32)
    sources = jnp.arange(doms, dtype=jnp.int32).astype(F32)[None, :]
    corrections = []
    for r in range(PAIR):
        mixing = jnp.zeros((doms, doms), F32)
        for k in range(6):
            mixing = mixing + jnp.where(
                listed[:, k : k + 1] == sources, weights[:, 2 * k + r : 2 * k + r + 1], 0.0
            )
        corrections.append(
            jnp.dot(
                mixing,
                got[:, 16 + r].astype(F32),
                precision=lax.Precision.HIGHEST,
                preferred_element_type=F32,
            )
        )
    correction = jnp.stack(corrections, axis=1).astype(BF16)
    sent = jnp.broadcast_to(correction[:, None], (doms, cols, PAIR, LANE))
    sent = sent.reshape(doms * cols, PAIR, LANE)
    arrived = lax.all_to_all(sent, ("dom", "col"), 0, 0, tiled=True)
    arrived = arrived.reshape(doms, cols, PAIR, LANE).transpose(1, 0, 2, 3)
    correction = arrived.reshape(cols, LIVE, LANE).astype(F32)
    loads = panel_loads.reshape(cols, MB, LANE)
    top = (loads[:, :LIVE].astype(F32) - live[None] * correction).astype(BF16)
    loaded = jnp.concatenate([top, loads[:, LIVE:]], axis=1).reshape(cols * MB, LANE)
    second_rows = jnp.dot(inverse_rows, loaded, preferred_element_type=F32).astype(BF16)

    pieces = [second_rows]
    quads = []
    for p in range(NPAN):
        owner = panel_block[p] // cols
        piece = lax.dynamic_slice(got, (owner, 0, 0), (1, 24, LANE))[0]
        pieces.append(piece[:16])
        quads.append(piece[18:19])
    pieces += quads + [jnp.zeros((14, LANE), BF16)]
    gathered = lax.all_gather(jnp.concatenate(pieces, axis=0), "col", axis=0, tiled=False)
    second = gathered[:, :MB].reshape(cols * MB, LANE)
    traces = jnp.dot(trace_map[0], second, preferred_element_type=F32).astype(BF16)

    picked = []
    for p in range(NPAN):
        lane = panel_block[p] % cols
        picked.append(lax.dynamic_slice(gathered, (lane, MB, 0), (1, 48, LANE))[0])
    shared = jnp.concatenate([picked[0][:16], picked[1][16:32]], axis=0)
    tail = jnp.concatenate([picked[0][32:33], picked[1][33:34], jnp.zeros((5, LANE), BF16)], axis=0)
    sent = jnp.concatenate(
        [
            jnp.broadcast_to(shared[None], (doms, 32, LANE)),
            traces[:, None],
            jnp.broadcast_to(tail[None], (doms, 7, LANE)),
        ],
        axis=1,
    )
    got = lax.all_to_all(sent, "dom", 0, 0, tiled=True)

    row_slots = surface_rows[0, 0].reshape(-1)
    landing = (jnp.arange(factor.shape[0], dtype=jnp.int32)[:, None] == row_slots[None, :]).astype(BF16)
    surface_sum = jnp.dot(landing, got[:, 32], preferred_element_type=F32)
    panels = []
    quads = []
    for p in range(NPAN):
        block = got[:, 16 * p : 16 * p + 16].reshape(4, 16, 16, LANE)
        panels.append(block.transpose(0, 2, 1, 3).reshape(P_SIZE, 16 * LANE))
        quads.append(join3(got[:, 33 + p, :48]))
    panel_factor = jnp.concatenate(panels, axis=0)
    quads = jnp.concatenate(quads, axis=0).T
    panel_points = quads[:12].reshape(3, 4, NPAN * P_SIZE)
    panel_weights = quads[12:]
    shifted = colloc[:, :, None, None] - panel_points[:, None, :, :]
    squared = jnp.sum(shifted * shifted, axis=0)
    green_values = jnp.cos(WAVE_NUMBER * jnp.sqrt(squared)) / (
        4.0 * math.pi * jnp.sqrt(squared + SMOOTHING * SMOOTHING)
    )
    kernel_block = jnp.sum(panel_weights[None, :, :] * green_values, axis=1)
    prior_update = lax.dot_general(
        factor_low, panel_factor, (((1,), (1,)), ((), ())), preferred_element_type=F32
    )
    return kernel_block - surface_sum - prior_update


def solution(mesh):
    in_specs = (
        P("dom", "col", None),
        P("dom", "col", None),
        P("dom", None, None),
        P("dom", None, "col"),
        P("dom", None),
        P(),
        P("dom", "col", None, None),
        P(("dom", "col"), None),
        P(None, ("dom", "col")),
        P(None, None, ("dom", "col")),
        P(None, ("dom", "col")),
        P(),
    )
    out_specs = P(("dom", "col"), None)
    return jax.shard_map(local, mesh=mesh, in_specs=in_specs, out_specs=out_specs, check_vma=False)
```

```python
import math

import jax
import jax.numpy as jnp
from jax import lax
from jax.sharding import PartitionSpec as P

MB = 208
P_SIZE = 64
NPAN = 2
LIVE = 128
MAX_LIVE = 112
PAIR = 2
LANE = 128

WAVE_NUMBER = 8.0
SMOOTHING = 0.05

F32 = jnp.float32
BF16 = jnp.bfloat16


def split3(values):
    high = lax.reduce_precision(values, 8, 7)
    rest = values - high
    middle = lax.reduce_precision(rest, 8, 7)
    low = rest - middle
    return jnp.concatenate(
        [high.astype(BF16), middle.astype(BF16), low.astype(BF16)], axis=-1
    )


def join3(parts):
    parts = parts.astype(F32)
    width = parts.shape[-1] // 3
    return (parts[..., 2 * width :] + parts[..., width : 2 * width]) + parts[..., :width]


def local(
    inverse,
    trace_map,
    panel_coupling,
    coupling,
    neighbours,
    iface_count,
    surface_rows,
    factor,
    colloc,
    quad_points,
    quad_weight,
    panel_block,
):
    dom_index = lax.axis_index("dom")
    doms = lax.axis_size("dom")
    cols = lax.axis_size("col")
    inverse_rows = inverse[0]
    panel_loads = panel_coupling[0]
    own_count = iface_count[dom_index]
    live = (jnp.arange(LIVE, dtype=jnp.int32) < own_count).astype(F32)[:, None]

    first_apply = jnp.dot(inverse_rows[:LIVE], panel_loads, preferred_element_type=F32)
    first_values = (first_apply * live).astype(BF16).reshape(doms, PAIR, LANE)
    factor_low = factor.astype(BF16)
    chunks = factor_low.reshape(4, 16, 16, LANE).transpose(0, 2, 1, 3).reshape(doms, 16, LANE)
    quads = jnp.concatenate([quad_points.reshape(12, P_SIZE), quad_weight], axis=0).T
    weights = coupling[0][:, :LIVE].reshape(6, doms, PAIR).transpose(1, 0, 2).reshape(doms, 12)
    listed = jnp.broadcast_to(neighbours.astype(F32).astype(BF16), (doms, 6))
    misc = jnp.concatenate(
        [split3(quads), split3(weights), listed, jnp.zeros((doms, LANE - 90), BF16)], axis=1
    )
    sent = jnp.concatenate(
        [chunks[:, :8], first_values, misc[:, None], jnp.zeros((doms, 5, LANE), BF16)], axis=1
    )
    sent, late = lax.optimization_barrier((sent, chunks[:, 8:]))
    got = lax.all_to_all(sent, "dom", 0, 0, tiled=True)

    misc = got[:, 10]
    weights = join3(misc[:, 48:84])
    listed = misc[:, 84:90].astype(F32)
    sources = jnp.arange(doms, dtype=jnp.int32).astype(F32)[None, :]
    corrections = []
    for r in range(PAIR):
        mixing = jnp.zeros((doms, doms), F32)
        for k in range(6):
            mixing = mixing + jnp.where(
                listed[:, k : k + 1] == sources, weights[:, 2 * k + r : 2 * k + r + 1], 0.0
            )
        corrections.append(
            jnp.dot(
                mixing,
                got[:, 8 + r].astype(F32),
                precision=lax.Precision.HIGHEST,
                preferred_element_type=F32,
            )
        )
    correction = jnp.stack(corrections, axis=1).astype(BF16)
    owners = [panel_block[p] // cols for p in range(NPAN)]
    lanes = [panel_block[p] % cols for p in range(NPAN)]
    early = [lax.dynamic_slice(got, (d, 0, 0), (1, 16, LANE))[0] for d in owners]
    sent = jnp.concatenate([late, correction, jnp.zeros((doms, 6, LANE), BF16)], axis=1)
    sent, early = lax.optimization_barrier((sent, early))
    got = lax.all_to_all(sent, "dom", 0, 0, tiled=True)

    arrived = got[:, 8:10].reshape(LIVE, LANE)
    finish = [lax.dynamic_slice(got, (d, 0, 0), (1, 16, LANE))[0] for d in owners]
    arrived, finish = lax.optimization_barrier((arrived, finish))
    correction = lax.all_gather(arrived[:MAX_LIVE], "col", axis=0, tiled=False).astype(F32)
    loads = panel_loads.reshape(cols, MB, LANE)
    top = loads[:, :MAX_LIVE].astype(F32) - live[None, :MAX_LIVE] * correction
    loaded = jnp.concatenate([top.astype(BF16), loads[:, MAX_LIVE:]], axis=1)
    loaded = loaded.reshape(cols * MB, LANE)
    second_rows = jnp.dot(inverse_rows, loaded, preferred_element_type=F32).astype(BF16)

    pieces = [second_rows]
    for p in range(NPAN):
        pieces += [early[p][:8], finish[p][:8]]
    pieces.append(jnp.concatenate([early[0][10:11, :48], early[1][10:11, :48], jnp.zeros((1, 32), BF16)], axis=1))
    pieces.append(jnp.zeros((15, LANE), BF16))
    gathered = lax.all_gather(jnp.concatenate(pieces, axis=0), "col", axis=0, tiled=False)
    second = gathered[:, :MB].reshape(cols * MB, LANE)
    traces = jnp.dot(trace_map[0], second, preferred_element_type=F32).astype(BF16)

    core = lax.axis_index("col") % 2
    own_lane = jnp.where(core == 0, lanes[0], lanes[1])
    shared = lax.dynamic_slice(gathered, (own_lane, MB + 16 * core, 0), (1, 16, LANE))[0]
    tails = [lax.dynamic_slice(gathered, (c, MB + 32, 0), (1, 1, LANE))[0] for c in lanes]
    tail = jnp.where(jnp.arange(LANE, dtype=jnp.int32)[None, :] < 48, tails[0], tails[1])
    last = jnp.stack([traces, jnp.broadcast_to(tail, (doms, LANE))], axis=1)
    sent = jnp.concatenate(
        [jnp.broadcast_to(shared.reshape(1, 8, 2, LANE), (doms, 8, 2, LANE)), last[:, None]], axis=1
    )
    got = lax.all_to_all(sent, "dom", 0, 0, tiled=True)

    tiles = got[:, :8].reshape(doms, 16, LANE)
    pairs = [(c, c ^ 1) for c in range(cols)]
    other = lax.ppermute(tiles, "col", pairs)
    row_slots = surface_rows[0, 0].reshape(-1)
    landing = (jnp.arange(factor.shape[0], dtype=jnp.int32)[:, None] == row_slots[None, :]).astype(BF16)
    surface_sum = jnp.dot(landing, got[:, 8, 0], preferred_element_type=F32)
    tail = got[:, 8, 1, :96].reshape(doms, NPAN, 48).transpose(1, 0, 2).reshape(NPAN * doms, 48)
    quads = join3(tail).T
    panel_points = quads[:12].reshape(3, 4, NPAN * P_SIZE)
    panel_weights = quads[12:]
    shifted = colloc[:, :, None, None] - panel_points[:, None, :, :]
    squared = jnp.sum(shifted * shifted, axis=0)
    green_values = jnp.cos(WAVE_NUMBER * jnp.sqrt(squared)) / (
        4.0 * math.pi * jnp.sqrt(squared + SMOOTHING * SMOOTHING)
    )
    kernel_block = jnp.sum(panel_weights[None, :, :] * green_values, axis=1)

    def prior(block):
        panel = block.reshape(4, 16, 16, LANE).transpose(0, 2, 1, 3).reshape(P_SIZE, 16 * LANE)
        return lax.dot_general(
            factor_low, panel, (((1,), (1,)), ((), ())), preferred_element_type=F32
        )

    own_part = prior(tiles)
    other_part = prior(other)
    prior_update = jnp.where(
        core == 0,
        jnp.concatenate([own_part, other_part], axis=1),
        jnp.concatenate([other_part, own_part], axis=1),
    )
    return kernel_block - surface_sum - prior_update


def solution(mesh):
    in_specs = (
        P("dom", "col", None),
        P("dom", "col", None),
        P("dom", None, None),
        P("dom", None, "col"),
        P("dom", None),
        P(),
        P("dom", "col", None, None),
        P(("dom", "col"), None),
        P(None, ("dom", "col")),
        P(None, None, ("dom", "col")),
        P(None, ("dom", "col")),
        P(),
    )
    out_specs = P(("dom", "col"), None)
    return jax.shard_map(local, mesh=mesh, in_specs=in_specs, out_specs=out_specs, check_vma=False)
```

```python
import math

import jax
import jax.numpy as jnp
from jax import lax
from jax.experimental import pallas as pl
from jax.experimental.pallas import tpu as pltpu
from jax.sharding import PartitionSpec as P

MB = 208
P_SIZE = 64
NPAN = 2
LIVE = 128
MAX_LIVE = 112
LANE = 128

WAVE_NUMBER = 8.0
SMOOTHING = 0.05

F32 = jnp.float32
BF16 = jnp.bfloat16
VM = pl.BlockSpec(memory_space=pltpu.VMEM)
SM = pl.BlockSpec(memory_space=pltpu.SMEM)
PARAMS = pltpu.CompilerParams(vmem_limit_bytes=16 * 1024 * 1024)


def iota(shape, axis):
    return lax.broadcasted_iota(jnp.int32, shape, axis)


def terms(values):
    high = values.astype(BF16).astype(F32)
    rest = values - high
    middle = rest.astype(BF16).astype(F32)
    return high, middle, rest - middle


def turned(left, right):
    return lax.dot_general(
        left, right.astype(BF16), (((1,), (1,)), ((), ())), preferred_element_type=F32
    )


def first_kernel(
    inv_hbm, map_hbm, loads_hbm, coup_hbm, listed_hbm, count_hbm, rows_hbm, factor_hbm, colloc_hbm,
    points_hbm, weight_hbm,
    sent_ref, late_ref, inv_ref, map_ref, loads_ref, low_ref, landing_ref, spots_ref,
    coup_in, listed_ref, count_ref, rows_ref, factor_ref, colloc_ref, points_ref, weight_ref,
    quad_ref, coup_scr, spot_scr, first_ref, row_ref, sems,
):
    doms = sent_ref.shape[0]
    moves = [
        pltpu.make_async_copy(src, dst, sems.at[i])
        for i, (src, dst) in enumerate(
            [
                (listed_hbm, listed_ref),
                (count_hbm, count_ref),
                (points_hbm, points_ref),
                (weight_hbm, weight_ref),
                (coup_hbm, coup_in),
                (rows_hbm, rows_ref),
                (colloc_hbm, colloc_ref),
                (factor_hbm, factor_ref),
                (loads_hbm, loads_ref),
                (inv_hbm, inv_ref),
                (map_hbm, map_ref),
            ]
        )
    ]
    for move in moves:
        move.start()
    coup_scr[...] = jnp.zeros_like(coup_scr)
    row_ref[...] = jnp.zeros_like(row_ref)
    spot_scr[...] = jnp.zeros_like(spot_scr)
    for move in moves[:7]:
        move.wait()
    count = count_ref[lax.axis_index("dom")]
    for c in range(3):
        quad_ref[4 * c : 4 * c + 4, :] = points_ref[c]
    quad_ref[12:16, :] = weight_ref[...]
    for k in range(6):
        coup_scr[k : k + 1, :] = coup_in[k][:, :LIVE]
    spot_scr[0:3, :] = colloc_ref[...]
    quads = jnp.concatenate(list(terms(quad_ref[...])) + [jnp.zeros((80, doms), F32)], axis=0)
    weights = list(terms(coup_scr[...]))
    even = jnp.concatenate([jnp.zeros((48, LIVE), F32)] + weights + [jnp.zeros((56, LIVE), F32)], axis=0)
    odd = jnp.concatenate([jnp.zeros((72, LIVE), F32)] + weights + [jnp.zeros((32, LIVE), F32)], axis=0)
    spots = jnp.concatenate(list(terms(spot_scr[...])) + [jnp.zeros((104, doms), F32)], axis=0)
    at = iota((doms, LIVE), 1)
    pair = 2 * iota((doms, LIVE), 0)
    unit = (iota((doms, doms), 0) == iota((doms, doms), 1)).astype(BF16)
    misc = turned(unit, quads)
    misc = misc + turned((at == pair).astype(BF16), even)
    misc = misc + turned((at == pair + 1).astype(BF16), odd)
    for k in range(6):
        misc = jnp.where(at == 96 + k, listed_ref[0, k].astype(F32), misc)
    misc = jnp.where(at == 102, count.astype(F32), misc)
    row_ref[pl.ds(2, doms, stride=8), :] = misc
    spots_ref[...] = turned(unit, spots)
    landing_ref[...] = (iota((doms, doms), 0) == rows_ref[0, 0]).astype(BF16)
    moves[7].wait()
    for h in range(doms):
        rows = pl.ds(8 * (h // 16), 8)
        lanes = pl.ds(LANE * (h % 16), LANE)
        sent_ref[h, :8, :] = factor_ref[rows, lanes].astype(BF16)
        rows = pl.ds(8 * (h // 16) + 32, 8)
        late_ref[h] = factor_ref[rows, lanes].astype(BF16)
    low_ref[...] = factor_ref[...].astype(BF16)
    for move in moves[8:10]:
        move.wait()
    first = jnp.dot(inv_ref[0, :LIVE, :], loads_ref[0], preferred_element_type=F32)
    first_ref[...] = jnp.where(iota((LIVE, LANE), 0) < count, first, 0.0)
    row_ref[pl.ds(0, doms, stride=8), :] = first_ref[pl.ds(0, doms, stride=2), :]
    row_ref[pl.ds(1, doms, stride=8), :] = first_ref[pl.ds(1, doms, stride=2), :]
    for h in range(doms):
        sent_ref[h, 8:16, :] = row_ref[8 * h : 8 * h + 8, :].astype(BF16)
    moves[10].wait()


def first_stage(
    inverse, trace_map, panel_coupling, coupling, neighbours, iface_count, surface_rows, factor,
    colloc, quad_points, quad_weight, doms,
):
    shape = jax.ShapeDtypeStruct
    coupling = coupling.transpose(1, 0, 2)
    return pl.pallas_call(
        first_kernel,
        out_shape=(
            shape((doms, 16, LANE), BF16),
            shape((doms, 8, LANE), BF16),
            shape(inverse.shape, BF16),
            shape(trace_map.shape, BF16),
            shape(panel_coupling.shape, BF16),
            shape(factor.shape, BF16),
            shape((doms, doms), BF16),
            shape((doms, LANE), F32),
        ),
        in_specs=[pl.BlockSpec(memory_space=pltpu.HBM)] * 11,
        out_specs=(VM,) * 8,
        scratch_shapes=[
            pltpu.VMEM(coupling.shape, F32),
            pltpu.SMEM(neighbours.shape, jnp.int32),
            pltpu.SMEM(iface_count.shape, jnp.int32),
            pltpu.VMEM(surface_rows.shape, jnp.int32),
            pltpu.VMEM(factor.shape, F32),
            pltpu.VMEM(colloc.shape, F32),
            pltpu.VMEM(quad_points.shape, F32),
            pltpu.VMEM(quad_weight.shape, F32),
            pltpu.VMEM((16, doms), F32),
            pltpu.VMEM((8, LIVE), F32),
            pltpu.VMEM((8, doms), F32),
            pltpu.VMEM((LIVE, LANE), F32),
            pltpu.VMEM((8 * doms, LANE), F32),
            pltpu.SemaphoreType.DMA((11,)),
        ],
        compiler_params=PARAMS,
        name="first_stage",
    )(
        *(
            pltpu.with_memory_space_constraint(x, pltpu.HBM)
            for x in (
                inverse, trace_map, panel_coupling, coupling, neighbours, iface_count, surface_rows,
                factor, colloc, quad_points, quad_weight,
            )
        )
    )


def mix_kernel(got_ref, late_ref, block_ref, sent_ref, early_ref, quad_ref, row_ref):
    doms = got_ref.shape[0]
    cols = lax.axis_size("col")
    for h in range(doms):
        row_ref[8 * h : 8 * h + 8, :] = got_ref[h, 8:16, :].astype(F32)
    misc = row_ref[pl.ds(2, doms, stride=8), :]
    weights = misc + pltpu.roll(misc, LANE - 8, 1) + pltpu.roll(misc, LANE - 16, 1)
    sources = iota((doms, doms), 1).astype(F32)
    mixed = []
    for r in range(2):
        mixing = jnp.zeros((doms, doms), F32)
        for k in range(6):
            lane = 48 + 24 * r + k
            mixing = mixing + jnp.where(
                misc[:, 96 + k : 97 + k] == sources, weights[:, lane : lane + 1], 0.0
            )
        summed = jnp.dot(
            mixing,
            row_ref[pl.ds(r, doms, stride=8), :],
            precision=lax.Precision.HIGHEST,
            preferred_element_type=F32,
        )
        row = (2 * lax.axis_index("dom") + r).astype(F32)
        mixed.append(jnp.where(misc[:, 102:103] > row, summed, 0.0))
    for p in range(NPAN):
        owner = block_ref[p] // cols
        early_ref[p] = got_ref[pl.ds(owner, 1)][0, :8, :]
        quad_ref[p] = got_ref[pl.ds(owner, 1)][0, 8:16, :]
    row_ref[pl.ds(0, doms, stride=8), :] = mixed[0]
    row_ref[pl.ds(1, doms, stride=8), :] = mixed[1]
    for h in range(doms):
        sent_ref[h, :8, :] = late_ref[h]
        sent_ref[h, 8:16, :] = row_ref[8 * h : 8 * h + 8, :].astype(BF16)


def mix_stage(got, late, panel_block):
    doms = got.shape[0]
    return pl.pallas_call(
        mix_kernel,
        out_shape=(
            jax.ShapeDtypeStruct((doms, 16, LANE), BF16),
            jax.ShapeDtypeStruct((NPAN, 8, LANE), BF16),
            jax.ShapeDtypeStruct((NPAN, 8, LANE), BF16),
        ),
        in_specs=[VM, VM, SM],
        out_specs=(VM, VM, VM),
        scratch_shapes=[pltpu.VMEM((8 * doms, LANE), F32)],
        compiler_params=PARAMS,
        name="mix_stage",
    )(got, late, panel_block)


def second_kernel(
    correction_ref, loads_ref, inv_ref, got_ref, early_ref, quad_ref, block_ref, out_ref, loaded_ref
):
    cols = correction_ref.shape[0]
    for c in range(cols):
        top = loads_ref[0, MB * c : MB * c + MAX_LIVE, :].astype(F32) - correction_ref[c].astype(F32)
        loaded_ref[MB * c : MB * c + MAX_LIVE, :] = top.astype(BF16)
        loaded_ref[MB * c + MAX_LIVE : MB * (c + 1), :] = loads_ref[0, MB * c + MAX_LIVE : MB * (c + 1), :]
    second = jnp.dot(inv_ref[0], loaded_ref[...], preferred_element_type=F32)
    out_ref[:MB, :] = second.astype(BF16)
    for p in range(NPAN):
        owner = lax.div(block_ref[p], cols)
        out_ref[MB + 16 * p : MB + 16 * p + 8, :] = early_ref[p]
        out_ref[MB + 16 * p + 8 : MB + 16 * p + 16, :] = got_ref[pl.ds(owner, 1)][0, :8, :]
        out_ref[MB + 32 + 8 * p : MB + 40 + 8 * p, :] = quad_ref[p]


def second_stage(correction, loads, inverse, got, early, quads, panel_block):
    return pl.pallas_call(
        second_kernel,
        out_shape=jax.ShapeDtypeStruct((MB + 48, LANE), BF16),
        in_specs=[VM] * 6 + [SM],
        out_specs=VM,
        scratch_shapes=[pltpu.VMEM(loads.shape[1:], BF16)],
        compiler_params=PARAMS,
        name="second_stage",
    )(correction, loads, inverse, got, early, quads, panel_block)


def trace_kernel(gathered_ref, map_ref, block_ref, shared_ref, last_ref, second_ref, row_ref):
    cols = gathered_ref.shape[0]
    doms = map_ref.shape[1]
    core = lax.rem(lax.axis_index("col"), 2)
    for c in range(cols):
        second_ref[MB * c : MB * (c + 1), :] = gathered_ref[c, :MB, :]
    traces = jnp.dot(map_ref[0], second_ref[...], preferred_element_type=F32)
    lanes = [lax.rem(block_ref[p], cols) for p in range(NPAN)]
    own = jnp.where(core == 0, lanes[0], lanes[1])
    first = gathered_ref[pl.ds(own, 1)][0, MB : MB + 16, :]
    second = gathered_ref[pl.ds(own, 1)][0, MB + 16 : MB + 32, :]
    shared_ref[...] = jnp.where(core == 0, first.astype(F32), second.astype(F32)).astype(BF16)
    quads = [
        gathered_ref[pl.ds(lanes[p], 1)][0, MB + 32 : MB + 48, :].astype(F32)[8 * p + 2 : 8 * p + 3, :]
        for p in range(NPAN)
    ]
    tail = jnp.where(iota((1, LANE), 1) < 48, quads[0], pltpu.roll(quads[1], 48, 1))
    row_ref[pl.ds(0, doms, stride=2), :] = traces
    row_ref[pl.ds(1, doms, stride=2), :] = jnp.broadcast_to(tail, (doms, LANE))
    last_ref[...] = row_ref[...].astype(BF16)


def trace_stage(gathered, trace_map, panel_block):
    doms = trace_map.shape[1]
    return pl.pallas_call(
        trace_kernel,
        out_shape=(
            jax.ShapeDtypeStruct((16, LANE), BF16),
            jax.ShapeDtypeStruct((2 * doms, LANE), BF16),
        ),
        in_specs=[VM, VM, SM],
        out_specs=(VM, VM),
        scratch_shapes=[
            pltpu.VMEM((trace_map.shape[2], LANE), BF16),
            pltpu.VMEM((2 * doms, LANE), F32),
        ],
        compiler_params=PARAMS,
        name="trace_stage",
    )(gathered, trace_map, panel_block)


def join3(parts):
    parts = parts.astype(F32)
    width = parts.shape[-1] // 3
    return (parts[..., 2 * width :] + parts[..., width : 2 * width]) + parts[..., :width]


def local(
    inverse,
    trace_map,
    panel_coupling,
    coupling,
    neighbours,
    iface_count,
    surface_rows,
    factor,
    colloc,
    quad_points,
    quad_weight,
    panel_block,
):
    doms = lax.axis_size("dom")
    cols = lax.axis_size("col")
    sent, late, inverse, trace_map, loads, factor_low, landing, spots = first_stage(
        inverse, trace_map, panel_coupling, coupling, neighbours, iface_count, surface_rows, factor,
        colloc, quad_points, quad_weight, doms,
    )
    got = lax.all_to_all(sent, "dom", 0, 0, tiled=True)
    sent, early, quads = mix_stage(got, late, panel_block)
    got = lax.all_to_all(sent, "dom", 0, 0, tiled=True)

    arrived = got[:, 8:10].reshape(LIVE, LANE)
    correction = lax.all_gather(arrived[:MAX_LIVE], "col", axis=0, tiled=False)
    pieces = second_stage(correction, loads, inverse, got, early, quads, panel_block)
    gathered = lax.all_gather(pieces, "col", axis=0, tiled=False)
    shared, last = trace_stage(gathered, trace_map, panel_block)

    core = lax.axis_index("col") % 2
    sent = jnp.concatenate(
        [
            jnp.broadcast_to(shared.reshape(1, 8, 2, LANE), (doms, 8, 2, LANE)),
            last.reshape(doms, 1, 2, LANE),
        ],
        axis=1,
    )
    got = lax.all_to_all(sent, "dom", 0, 0, tiled=True)

    tiles = got[:, :8].reshape(doms, 16, LANE)
    pairs = [(c, c ^ 1) for c in range(cols)]
    other = lax.ppermute(tiles, "col", pairs)
    surface_sum = jnp.dot(landing, got[:, 8, 0], preferred_element_type=F32)
    tail = got[:, 8, 1, :96].reshape(doms, NPAN, 48).transpose(1, 0, 2).reshape(NPAN * doms, 48)
    quads = join3(tail).T
    panel_points = quads[:12].reshape(3, 4, NPAN * P_SIZE)
    panel_weights = quads[12:]
    spots = (spots[:, 16:19] + spots[:, 8:11]) + spots[:, 0:3]
    shifted = spots.T[:, :, None, None] - panel_points[:, None, :, :]
    squared = jnp.sum(shifted * shifted, axis=0)
    green_values = jnp.cos(WAVE_NUMBER * jnp.sqrt(squared)) / (
        4.0 * math.pi * jnp.sqrt(squared + SMOOTHING * SMOOTHING)
    )
    kernel_block = jnp.sum(panel_weights[None, :, :] * green_values, axis=1)

    def prior(block):
        panel = block.reshape(4, 16, 2, 8, LANE).transpose(2, 0, 3, 1, 4).reshape(P_SIZE, 16 * LANE)
        return lax.dot_general(
            factor_low, panel, (((1,), (1,)), ((), ())), preferred_element_type=F32
        )

    own_part = prior(tiles)
    other_part = prior(other)
    prior_update = jnp.where(
        core == 0,
        jnp.concatenate([own_part, other_part], axis=1),
        jnp.concatenate([other_part, own_part], axis=1),
    )
    return kernel_block - surface_sum - prior_update


def solution(mesh):
    in_specs = (
        P("dom", "col", None),
        P("dom", "col", None),
        P("dom", None, None),
        P("dom", None, "col"),
        P("dom", None),
        P(),
        P("dom", "col", None, None),
        P(("dom", "col"), None),
        P(None, ("dom", "col")),
        P(None, None, ("dom", "col")),
        P(None, ("dom", "col")),
        P(),
    )
    out_specs = P(("dom", "col"), None)
    return jax.shard_map(local, mesh=mesh, in_specs=in_specs, out_specs=out_specs, check_vma=False)
```

```python
import math

import jax
import jax.numpy as jnp
from jax import lax
from jax.experimental import pallas as pl
from jax.experimental.pallas import tpu as pltpu
from jax.sharding import PartitionSpec as P

MB = 208
P_SIZE = 64
NPAN = 2
LIVE = 128
MAX_LIVE = 112
LANE = 128
ROWS = 20

WAVE_NUMBER = 8.0
SMOOTHING = 0.05

F32 = jnp.float32
BF16 = jnp.bfloat16
VM = pl.BlockSpec(memory_space=pltpu.VMEM)
PARAMS = pltpu.CompilerParams(vmem_limit_bytes=16 * 1024 * 1024)


def iota(shape, axis):
    return lax.broadcasted_iota(jnp.int32, shape, axis)


def terms(values):
    high = values.astype(BF16).astype(F32)
    rest = values - high
    middle = rest.astype(BF16).astype(F32)
    return high, middle, rest - middle


def turned(left, right):
    return lax.dot_general(
        left, right.astype(BF16), (((1,), (1,)), ((), ())), preferred_element_type=F32
    )


def first_kernel(
    inv_hbm, map_hbm, loads_hbm, coup_hbm, listed_hbm, count_hbm, rows_hbm, factor_hbm, colloc_hbm,
    points_hbm, weight_hbm,
    sent_ref, inv_ref, map_ref, loads_ref, low_ref, landing_ref, spots_ref,
    coup_in, listed_ref, count_ref, rows_ref, factor_ref, colloc_ref, points_ref, weight_ref,
    quad_ref, coup_scr, spot_scr, first_ref, row_ref, sems,
):
    doms = landing_ref.shape[1]
    moves = [
        pltpu.make_async_copy(src, dst, sems.at[i])
        for i, (src, dst) in enumerate(
            [
                (listed_hbm, listed_ref),
                (count_hbm, count_ref),
                (points_hbm, points_ref),
                (weight_hbm, weight_ref),
                (coup_hbm, coup_in),
                (rows_hbm, rows_ref),
                (colloc_hbm, colloc_ref),
                (factor_hbm, factor_ref),
                (loads_hbm, loads_ref),
                (inv_hbm, inv_ref),
                (map_hbm, map_ref),
            ]
        )
    ]
    for move in moves:
        move.start()
    coup_scr[...] = jnp.zeros_like(coup_scr)
    row_ref[...] = jnp.zeros_like(row_ref)
    spot_scr[...] = jnp.zeros_like(spot_scr)
    for move in moves[:7]:
        move.wait()
    count = count_ref[lax.axis_index("dom")]
    for c in range(3):
        quad_ref[4 * c : 4 * c + 4, :] = points_ref[c]
    quad_ref[12:16, :] = weight_ref[...]
    for k in range(6):
        coup_scr[k : k + 1, :] = coup_in[k][:, :LIVE]
    spot_scr[0:3, :] = colloc_ref[...]
    quads = jnp.concatenate(list(terms(quad_ref[...])) + [jnp.zeros((80, doms), F32)], axis=0)
    weights = list(terms(coup_scr[...]))
    even = jnp.concatenate([jnp.zeros((48, LIVE), F32)] + weights + [jnp.zeros((56, LIVE), F32)], axis=0)
    odd = jnp.concatenate([jnp.zeros((72, LIVE), F32)] + weights + [jnp.zeros((32, LIVE), F32)], axis=0)
    spots = jnp.concatenate(list(terms(spot_scr[...])) + [jnp.zeros((104, doms), F32)], axis=0)
    at = iota((doms, LIVE), 1)
    pair = 2 * iota((doms, LIVE), 0)
    unit = (iota((doms, doms), 0) == iota((doms, doms), 1)).astype(BF16)
    misc = turned(unit, quads)
    misc = misc + turned((at == pair).astype(BF16), even)
    misc = misc + turned((at == pair + 1).astype(BF16), odd)
    for k in range(6):
        misc = jnp.where(at == 96 + k, listed_ref[0, k].astype(F32), misc)
    misc = jnp.where(at == 102, count.astype(F32), misc)
    row_ref[pl.ds(2, doms, stride=4), :] = misc
    spots = turned(unit, spots)
    spots_ref[...] = spots + pltpu.roll(spots, LANE - 8, 1) + pltpu.roll(spots, LANE - 16, 1)
    landing_ref[...] = (iota((doms, doms), 0) == rows_ref[0, 0]).astype(BF16)
    moves[7].wait()
    for h in range(doms):
        tile = factor_ref[pl.ds(16 * (h // 16), 16), pl.ds(LANE * (h % 16), LANE)]
        sent_ref[ROWS * h : ROWS * h + 16, :] = tile.astype(BF16)
    low_ref[...] = factor_ref[...].astype(BF16)
    for move in moves[8:10]:
        move.wait()
    first = jnp.dot(inv_ref[0, :LIVE, :], loads_ref[0], preferred_element_type=F32)
    first_ref[...] = jnp.where(iota((LIVE, LANE), 0) < count, first, 0.0)
    row_ref[pl.ds(0, doms, stride=4), :] = first_ref[pl.ds(0, doms, stride=2), :]
    row_ref[pl.ds(1, doms, stride=4), :] = first_ref[pl.ds(1, doms, stride=2), :]
    for h in range(doms):
        sent_ref[ROWS * h + 16 : ROWS * h + 20, :] = row_ref[4 * h : 4 * h + 4, :].astype(BF16)
    moves[10].wait()


def first_stage(
    inverse, trace_map, panel_coupling, coupling, neighbours, iface_count, surface_rows, factor,
    colloc, quad_points, quad_weight, doms,
):
    shape = jax.ShapeDtypeStruct
    coupling = coupling.transpose(1, 0, 2)
    return pl.pallas_call(
        first_kernel,
        out_shape=(
            shape((ROWS * doms, LANE), BF16),
            shape(inverse.shape, BF16),
            shape(trace_map.shape, BF16),
            shape(panel_coupling.shape, BF16),
            shape(factor.shape, BF16),
            shape((doms, doms), BF16),
            shape((doms, LANE), F32),
        ),
        in_specs=[pl.BlockSpec(memory_space=pltpu.HBM)] * 11,
        out_specs=(VM,) * 7,
        scratch_shapes=[
            pltpu.VMEM(coupling.shape, F32),
            pltpu.SMEM(neighbours.shape, jnp.int32),
            pltpu.SMEM(iface_count.shape, jnp.int32),
            pltpu.VMEM(surface_rows.shape, jnp.int32),
            pltpu.VMEM(factor.shape, F32),
            pltpu.VMEM(colloc.shape, F32),
            pltpu.VMEM(quad_points.shape, F32),
            pltpu.VMEM(quad_weight.shape, F32),
            pltpu.VMEM((16, doms), F32),
            pltpu.VMEM((8, LIVE), F32),
            pltpu.VMEM((8, doms), F32),
            pltpu.VMEM((LIVE, LANE), F32),
            pltpu.VMEM((4 * doms, LANE), F32),
            pltpu.SemaphoreType.DMA((11,)),
        ],
        compiler_params=PARAMS,
        name="first_stage",
    )(
        *(
            pltpu.with_memory_space_constraint(x, pltpu.HBM)
            for x in (
                inverse, trace_map, panel_coupling, coupling, neighbours, iface_count, surface_rows,
                factor, colloc, quad_points, quad_weight,
            )
        )
    )


def mix_kernel(got_ref, pair_ref, block_hbm, sent_ref, picks_ref, block_ref, row_ref, sem):
    doms = pair_ref.shape[0]
    cols = sent_ref.shape[0]
    move = pltpu.make_async_copy(block_hbm, block_ref, sem.at[0])
    move.start()
    for h in range(doms):
        row_ref[4 * h : 4 * h + 4, :] = got_ref[ROWS * h + 16 : ROWS * h + 20, :].astype(F32)
    misc = row_ref[pl.ds(2, doms, stride=4), :]
    weights = misc + pltpu.roll(misc, LANE - 8, 1) + pltpu.roll(misc, LANE - 16, 1)
    sources = iota((doms, doms), 1).astype(F32)
    mixed = []
    for r in range(2):
        mixing = jnp.zeros((doms, doms), F32)
        for k in range(6):
            lane = 48 + 24 * r + k
            mixing = mixing + jnp.where(
                misc[:, 96 + k : 97 + k] == sources, weights[:, lane : lane + 1], 0.0
            )
        summed = jnp.dot(
            mixing,
            row_ref[pl.ds(r, doms, stride=4), :],
            precision=lax.Precision.HIGHEST,
            preferred_element_type=F32,
        )
        row = (2 * lax.axis_index("dom") + r).astype(F32)
        mixed.append(jnp.where(misc[:, 102:103] > row, summed, 0.0))
    row_ref[pl.ds(0, doms, stride=2), :] = mixed[0]
    row_ref[pl.ds(1, doms, stride=2), :] = mixed[1]
    correction = row_ref[: 2 * doms, :].astype(BF16)
    for c in range(cols):
        sent_ref[c] = correction
    move.wait()
    for p in range(NPAN):
        owner = lax.div(block_ref[p], cols)
        picks_ref[p] = pair_ref[pl.ds(owner, 1)][0]


def mix_stage(got, panel_block, doms, cols):
    return pl.pallas_call(
        mix_kernel,
        out_shape=(
            jax.ShapeDtypeStruct((cols, 2 * doms, LANE), BF16),
            jax.ShapeDtypeStruct((NPAN, ROWS // 2, 2, LANE), BF16),
        ),
        in_specs=[VM, VM, pl.BlockSpec(memory_space=pltpu.HBM)],
        out_specs=(VM, VM),
        scratch_shapes=[
            pltpu.SMEM(panel_block.shape, jnp.int32),
            pltpu.VMEM((4 * doms, LANE), F32),
            pltpu.SemaphoreType.DMA((1,)),
        ],
        compiler_params=PARAMS,
        name="mix_stage",
    )(
        got.reshape(ROWS * doms, LANE),
        got,
        pltpu.with_memory_space_constraint(panel_block, pltpu.HBM),
    )


def second_kernel(correction_ref, loads_ref, inv_ref, picks_ref, out_ref, loaded_ref):
    cols = correction_ref.shape[0]
    for c in range(cols):
        top = loads_ref[0, MB * c : MB * c + MAX_LIVE, :].astype(F32)
        top = top - correction_ref[c, :MAX_LIVE, :].astype(F32)
        loaded_ref[MB * c : MB * c + MAX_LIVE, :] = top.astype(BF16)
        loaded_ref[MB * c + MAX_LIVE : MB * (c + 1), :] = loads_ref[0, MB * c + MAX_LIVE : MB * (c + 1), :]
    second = jnp.dot(inv_ref[0], loaded_ref[...], preferred_element_type=F32)
    out_ref[:MB, :] = second.astype(BF16)
    out_ref[MB + 32 :, :] = jnp.zeros((16, LANE), BF16)
    for p in range(NPAN):
        out_ref[MB + 16 * p : MB + 16 * p + 16, :] = picks_ref[ROWS * p : ROWS * p + 16, :]
        out_ref[MB + 32 + 2 * p : MB + 34 + 2 * p, :] = picks_ref[ROWS * p + 18 : ROWS * p + 20, :]


def second_stage(correction, loads, inverse, picks):
    return pl.pallas_call(
        second_kernel,
        out_shape=jax.ShapeDtypeStruct((MB + 48, LANE), BF16),
        in_specs=[VM] * 4,
        out_specs=VM,
        scratch_shapes=[pltpu.VMEM(loads.shape[1:], BF16)],
        compiler_params=PARAMS,
        name="second_stage",
    )(correction, loads, inverse, picks.reshape(NPAN * ROWS, LANE))


def trace_kernel(
    gathered_ref, map_ref, block_hbm, shared_ref, last_ref, block_ref, second_ref, row_ref, sem
):
    move = pltpu.make_async_copy(block_hbm, block_ref, sem.at[0])
    move.start()
    cols = gathered_ref.shape[0]
    doms = map_ref.shape[1]
    core = lax.rem(lax.axis_index("col"), 2)
    for c in range(cols):
        second_ref[MB * c : MB * (c + 1), :] = gathered_ref[c, :MB, :]
    traces = jnp.dot(map_ref[0], second_ref[...], preferred_element_type=F32)
    move.wait()
    lanes = [lax.rem(block_ref[p], cols) for p in range(NPAN)]
    own = jnp.where(core == 0, lanes[0], lanes[1])
    first = gathered_ref[pl.ds(own, 1)][0, MB : MB + 16, :]
    second = gathered_ref[pl.ds(own, 1)][0, MB + 16 : MB + 32, :]
    shared_ref[...] = jnp.where(core == 0, first.astype(F32), second.astype(F32)).astype(BF16)
    quads = [
        gathered_ref[pl.ds(lanes[p], 1)][0, MB + 32 : MB + 48, :].astype(F32)[2 * p : 2 * p + 1, :]
        for p in range(NPAN)
    ]
    tail = jnp.where(iota((1, LANE), 1) < 48, quads[0], pltpu.roll(quads[1], 48, 1))
    row_ref[pl.ds(0, doms, stride=2), :] = traces
    row_ref[pl.ds(1, doms, stride=2), :] = jnp.broadcast_to(tail, (doms, LANE))
    last_ref[...] = row_ref[...].astype(BF16)


def trace_stage(gathered, trace_map, panel_block):
    doms = trace_map.shape[1]
    return pl.pallas_call(
        trace_kernel,
        out_shape=(
            jax.ShapeDtypeStruct((16, LANE), BF16),
            jax.ShapeDtypeStruct((2 * doms, LANE), BF16),
        ),
        in_specs=[VM, VM, pl.BlockSpec(memory_space=pltpu.HBM)],
        out_specs=(VM, VM),
        scratch_shapes=[
            pltpu.SMEM(panel_block.shape, jnp.int32),
            pltpu.VMEM((trace_map.shape[2], LANE), BF16),
            pltpu.VMEM((2 * doms, LANE), F32),
            pltpu.SemaphoreType.DMA((1,)),
        ],
        compiler_params=PARAMS,
        name="trace_stage",
    )(gathered, trace_map, pltpu.with_memory_space_constraint(panel_block, pltpu.HBM))


def panel_of(block_ref, panel_ref, doms):
    for h in range(doms):
        tile = block_ref[18 * h : 18 * h + 16, :]
        panel_ref[pl.ds(16 * (h // 16), 16), pl.ds(LANE * (h % 16), LANE)] = tile


def placed(low_ref, panel_ref, side):
    prior = lax.dot_general(
        low_ref[...], panel_ref[...], (((1,), (1,)), ((), ())), preferred_element_type=F32
    )
    both = jnp.concatenate([prior, prior], axis=1)
    return jnp.where((iota(both.shape, 1) >= P_SIZE) == (side == 1), both, 0.0)


def near_kernel(block_ref, low_ref, landing_ref, spots_ref, base_ref, panel_ref, row_ref):
    doms = landing_ref.shape[1]
    core = lax.rem(lax.axis_index("col"), 2)
    for h in range(doms):
        row_ref[2 * h : 2 * h + 2, :] = block_ref[18 * h + 16 : 18 * h + 18, :].astype(F32)
    traces = row_ref[pl.ds(0, doms, stride=2), :].astype(BF16)
    tails = row_ref[pl.ds(1, doms, stride=2), :]
    surface = jnp.dot(landing_ref[...], traces, preferred_element_type=F32)
    halves = []
    for p in range(NPAN):
        parts = []
        for t in range(3):
            pick = iota((16, LANE), 1) == iota((16, LANE), 0) + (48 * p + 16 * t)
            parts.append(turned(pick.astype(BF16), tails))
        halves.append((parts[2] + parts[1]) + parts[0])
    quads = jnp.concatenate(halves, axis=1)
    kernel_block = jnp.zeros_like(surface)
    for b in range(4):
        squared = jnp.zeros_like(surface)
        for c in range(3):
            shifted = spots_ref[:, c : c + 1] - quads[4 * c + b : 4 * c + b + 1, :]
            squared = squared + shifted * shifted
        green = jnp.cos(WAVE_NUMBER * jnp.sqrt(squared)) / (
            4.0 * math.pi * jnp.sqrt(squared + SMOOTHING * SMOOTHING)
        )
        kernel_block = kernel_block + quads[12 + b : 13 + b, :] * green
    panel_of(block_ref, panel_ref, doms)
    base_ref[...] = kernel_block - surface - placed(low_ref, panel_ref, core)


def far_kernel(block_ref, low_ref, base_ref, out_ref, panel_ref):
    core = lax.rem(lax.axis_index("col"), 2)
    panel_of(block_ref, panel_ref, block_ref.shape[0] // 18)
    out_ref[...] = base_ref[...] - placed(low_ref, panel_ref, 1 - core)


def near_stage(block, low, landing, spots):
    return pl.pallas_call(
        near_kernel,
        out_shape=jax.ShapeDtypeStruct((low.shape[0], LANE), F32),
        in_specs=[VM] * 4,
        out_specs=VM,
        scratch_shapes=[
            pltpu.VMEM(low.shape, BF16),
            pltpu.VMEM((2 * landing.shape[1], LANE), F32),
        ],
        compiler_params=PARAMS,
        cost_estimate=pl.CostEstimate(flops=40_000_000, bytes_accessed=1_000_000, transcendentals=100_000),
        name="near_stage",
    )(block, low, landing, spots)


def far_stage(block, low, base):
    return pl.pallas_call(
        far_kernel,
        out_shape=jax.ShapeDtypeStruct(base.shape, F32),
        in_specs=[VM] * 3,
        out_specs=VM,
        scratch_shapes=[pltpu.VMEM(low.shape, BF16)],
        compiler_params=PARAMS,
        name="far_stage",
    )(block, low, base)


def local(
    inverse,
    trace_map,
    panel_coupling,
    coupling,
    neighbours,
    iface_count,
    surface_rows,
    factor,
    colloc,
    quad_points,
    quad_weight,
    panel_block,
):
    doms = lax.axis_size("dom")
    cols = lax.axis_size("col")
    sent, inverse, trace_map, loads, factor_low, landing, spots = first_stage(
        inverse, trace_map, panel_coupling, coupling, neighbours, iface_count, surface_rows, factor,
        colloc, quad_points, quad_weight, doms,
    )
    got = lax.all_to_all(sent.reshape(doms, ROWS // 2, 2, LANE), "dom", 0, 0, tiled=True)
    sent, picks = mix_stage(got, panel_block, doms, cols)

    sent = sent.reshape(cols * doms, 2, LANE)
    correction = lax.all_to_all(sent, ("col", "dom"), 0, 0, tiled=True)
    correction = correction.reshape(cols, 2 * doms, LANE)
    pieces = second_stage(correction, loads, inverse, picks)
    gathered = lax.all_gather(pieces, "col", axis=0, tiled=False)
    shared, last = trace_stage(gathered, trace_map, panel_block)

    sent = jnp.concatenate(
        [
            jnp.broadcast_to(shared.reshape(1, 8, 2, LANE), (doms, 8, 2, LANE)),
            last.reshape(doms, 1, 2, LANE),
        ],
        axis=1,
    )
    got = lax.all_to_all(sent, "dom", 0, 0, tiled=True)
    other = lax.ppermute(got, "col", [(c, c ^ 1) for c in range(cols)])
    base = near_stage(got.reshape(18 * doms, LANE), factor_low, landing, spots)
    return far_stage(other.reshape(18 * doms, LANE), factor_low, base)


def solution(mesh):
    in_specs = (
        P("dom", "col", None),
        P("dom", "col", None),
        P("dom", None, None),
        P("dom", None, "col"),
        P("dom", None),
        P(),
        P("dom", "col", None, None),
        P(("dom", "col"), None),
        P(None, ("dom", "col")),
        P(None, None, ("dom", "col")),
        P(None, ("dom", "col")),
        P(),
    )
    out_specs = P(("dom", "col"), None)
    return jax.shard_map(local, mesh=mesh, in_specs=in_specs, out_specs=out_specs, check_vma=False)
```

```python
import math

import jax
import jax.numpy as jnp
from jax import lax
from jax.experimental import pallas as pl
from jax.experimental.pallas import tpu as pltpu
from jax.sharding import PartitionSpec as P

MB = 208
P_SIZE = 64
NPAN = 2
LIVE = 128
MAX_LIVE = 112
LANE = 128
ROWS = 4
PIECE = 224

WAVE_NUMBER = 8.0
SMOOTHING = 0.05

F32 = jnp.float32
BF16 = jnp.bfloat16
VM = pl.BlockSpec(memory_space=pltpu.VMEM)
PARAMS = pltpu.CompilerParams(vmem_limit_bytes=16 * 1024 * 1024)


def iota(shape, axis):
    return lax.broadcasted_iota(jnp.int32, shape, axis)


def terms(values):
    high = values.astype(BF16).astype(F32)
    rest = values - high
    middle = rest.astype(BF16).astype(F32)
    return high, middle, rest - middle


def turned(left, right):
    return lax.dot_general(
        left, right.astype(BF16), (((1,), (1,)), ((), ())), preferred_element_type=F32
    )


def first_kernel(
    inv_hbm, map_hbm, loads_hbm, coup_hbm, listed_hbm, count_hbm, rows_hbm, factor_hbm, colloc_hbm,
    points_hbm, weight_hbm,
    sent_ref, inv_ref, map_ref, loads_ref, low_ref, landing_ref, spots_ref,
    coup_in, listed_ref, count_ref, rows_ref, factor_ref, colloc_ref, points_ref, weight_ref,
    quad_ref, coup_scr, spot_scr, first_ref, row_ref, sems,
):
    doms = landing_ref.shape[1]
    moves = [
        pltpu.make_async_copy(src, dst, sems.at[i])
        for i, (src, dst) in enumerate(
            [
                (listed_hbm, listed_ref),
                (count_hbm, count_ref),
                (points_hbm, points_ref),
                (weight_hbm, weight_ref),
                (coup_hbm, coup_in),
                (rows_hbm, rows_ref),
                (colloc_hbm, colloc_ref),
                (factor_hbm, factor_ref),
                (loads_hbm, loads_ref),
                (inv_hbm, inv_ref),
                (map_hbm, map_ref),
            ]
        )
    ]
    for move in moves:
        move.start()
    coup_scr[...] = jnp.zeros_like(coup_scr)
    row_ref[...] = jnp.zeros_like(row_ref)
    spot_scr[...] = jnp.zeros_like(spot_scr)
    for move in moves[:7]:
        move.wait()
    count = count_ref[lax.axis_index("dom")]
    for c in range(3):
        quad_ref[4 * c : 4 * c + 4, :] = points_ref[c]
    quad_ref[12:16, :] = weight_ref[...]
    for k in range(6):
        coup_scr[k : k + 1, :] = coup_in[k][:, :LIVE]
    spot_scr[0:3, :] = colloc_ref[...]
    quads = jnp.concatenate(list(terms(quad_ref[...])) + [jnp.zeros((80, doms), F32)], axis=0)
    weights = list(terms(coup_scr[...]))
    even = jnp.concatenate([jnp.zeros((48, LIVE), F32)] + weights + [jnp.zeros((56, LIVE), F32)], axis=0)
    odd = jnp.concatenate([jnp.zeros((72, LIVE), F32)] + weights + [jnp.zeros((32, LIVE), F32)], axis=0)
    spots = jnp.concatenate(list(terms(spot_scr[...])) + [jnp.zeros((104, doms), F32)], axis=0)
    at = iota((doms, LIVE), 1)
    pair = 2 * iota((doms, LIVE), 0)
    unit = (iota((doms, doms), 0) == iota((doms, doms), 1)).astype(BF16)
    misc = turned(unit, quads)
    misc = misc + turned((at == pair).astype(BF16), even)
    misc = misc + turned((at == pair + 1).astype(BF16), odd)
    for k in range(6):
        misc = jnp.where(at == 96 + k, listed_ref[0, k].astype(F32), misc)
    misc = jnp.where(at == 102, count.astype(F32), misc)
    row_ref[pl.ds(2, doms, stride=4), :] = misc
    spots = turned(unit, spots)
    spots_ref[...] = spots + pltpu.roll(spots, LANE - 8, 1) + pltpu.roll(spots, LANE - 16, 1)
    landing_ref[...] = (iota((doms, doms), 0) == rows_ref[0, 0]).astype(BF16)
    moves[7].wait()
    low_ref[...] = factor_ref[...].astype(BF16)
    for move in moves[8:10]:
        move.wait()
    first = jnp.dot(inv_ref[0, :LIVE, :], loads_ref[0], preferred_element_type=F32)
    first_ref[...] = jnp.where(iota((LIVE, LANE), 0) < count, first, 0.0)
    row_ref[pl.ds(0, doms, stride=4), :] = first_ref[pl.ds(0, doms, stride=2), :]
    row_ref[pl.ds(1, doms, stride=4), :] = first_ref[pl.ds(1, doms, stride=2), :]
    sent_ref[...] = row_ref[...].astype(BF16)
    moves[10].wait()


def first_stage(
    inverse, trace_map, panel_coupling, coupling, neighbours, iface_count, surface_rows, factor,
    colloc, quad_points, quad_weight, doms,
):
    shape = jax.ShapeDtypeStruct
    coupling = coupling.transpose(1, 0, 2)
    return pl.pallas_call(
        first_kernel,
        out_shape=(
            shape((ROWS * doms, LANE), BF16),
            shape(inverse.shape, BF16),
            shape(trace_map.shape, BF16),
            shape(panel_coupling.shape, BF16),
            shape(factor.shape, BF16),
            shape((doms, doms), BF16),
            shape((doms, LANE), F32),
        ),
        in_specs=[pl.BlockSpec(memory_space=pltpu.HBM)] * 11,
        out_specs=(VM,) * 7,
        scratch_shapes=[
            pltpu.VMEM(coupling.shape, F32),
            pltpu.SMEM(neighbours.shape, jnp.int32),
            pltpu.SMEM(iface_count.shape, jnp.int32),
            pltpu.VMEM(surface_rows.shape, jnp.int32),
            pltpu.VMEM(factor.shape, F32),
            pltpu.VMEM(colloc.shape, F32),
            pltpu.VMEM(quad_points.shape, F32),
            pltpu.VMEM(quad_weight.shape, F32),
            pltpu.VMEM((16, doms), F32),
            pltpu.VMEM((8, LIVE), F32),
            pltpu.VMEM((8, doms), F32),
            pltpu.VMEM((LIVE, LANE), F32),
            pltpu.VMEM((4 * doms, LANE), F32),
            pltpu.SemaphoreType.DMA((11,)),
        ],
        compiler_params=PARAMS,
        name="first_stage",
    )(
        *(
            pltpu.with_memory_space_constraint(x, pltpu.HBM)
            for x in (
                inverse, trace_map, panel_coupling, coupling, neighbours, iface_count, surface_rows,
                factor, colloc, quad_points, quad_weight,
            )
        )
    )


def mix_kernel(got_ref, pair_ref, low_ref, block_hbm, sent_ref, quad_ref, block_ref, row_ref, work_ref, sem):
    doms = pair_ref.shape[0]
    cols = sent_ref.shape[0] // (ROWS * doms)
    move = pltpu.make_async_copy(block_hbm, block_ref, sem.at[0])
    move.start()
    row_ref[...] = got_ref[...].astype(F32)
    for t in range(2 * doms):
        tile = low_ref[pl.ds(8 * (t // 16), 8), pl.ds(LANE * (t % 16), LANE)]
        work_ref[pl.ds(ROWS * (t // 2) + 2 + t % 2, cols, stride=ROWS * doms), :] = tile.astype(F32)
    misc = row_ref[pl.ds(2, doms, stride=ROWS), :]
    weights = misc + pltpu.roll(misc, LANE - 8, 1) + pltpu.roll(misc, LANE - 16, 1)
    sources = iota((doms, doms), 1).astype(F32)
    for r in range(2):
        mixing = jnp.zeros((doms, doms), F32)
        for k in range(6):
            lane = 48 + 24 * r + k
            mixing = mixing + jnp.where(
                misc[:, 96 + k : 97 + k] == sources, weights[:, lane : lane + 1], 0.0
            )
        summed = jnp.dot(
            mixing,
            row_ref[pl.ds(r, doms, stride=ROWS), :],
            precision=lax.Precision.HIGHEST,
            preferred_element_type=F32,
        )
        row = (2 * lax.axis_index("dom") + r).astype(F32)
        summed = jnp.where(misc[:, 102:103] > row, summed, 0.0)
        for c in range(cols):
            work_ref[pl.ds(ROWS * doms * c + r, doms, stride=ROWS), :] = summed
    sent_ref[...] = work_ref[...].astype(BF16)
    move.wait()
    for p in range(NPAN):
        owner = lax.div(block_ref[p], cols)
        quad_ref[p] = pair_ref[pl.ds(owner, 1)][0, 1]


def mix_stage(got, low, panel_block, doms, cols):
    return pl.pallas_call(
        mix_kernel,
        out_shape=(
            jax.ShapeDtypeStruct((ROWS * doms * cols, LANE), BF16),
            jax.ShapeDtypeStruct((NPAN, 2, LANE), BF16),
        ),
        in_specs=[VM, VM, VM, pl.BlockSpec(memory_space=pltpu.HBM)],
        out_specs=(VM, VM),
        scratch_shapes=[
            pltpu.SMEM(panel_block.shape, jnp.int32),
            pltpu.VMEM((ROWS * doms, LANE), F32),
            pltpu.VMEM((ROWS * doms * cols, LANE), F32),
            pltpu.SemaphoreType.DMA((1,)),
        ],
        compiler_params=PARAMS,
        name="mix_stage",
    )(
        got.reshape(ROWS * doms, LANE),
        got,
        low,
        pltpu.with_memory_space_constraint(panel_block, pltpu.HBM),
    )


def second_kernel(
    got_ref, pair_ref, loads_ref, inv_ref, quad_ref, block_hbm, out_ref, block_ref, work_ref, loaded_ref, sem
):
    cols = lax.axis_size("col")
    doms = pair_ref.shape[0] // cols
    move = pltpu.make_async_copy(block_hbm, block_ref, sem.at[0])
    move.start()
    loaded_ref[...] = loads_ref[0].astype(F32)
    work_ref[...] = got_ref[...].astype(F32)
    for c in range(cols):
        for r in range(2):
            rows = pl.ds(MB * c + r, MAX_LIVE // 2, stride=2)
            correction = work_ref[pl.ds(ROWS * doms * c + r, MAX_LIVE // 2, stride=ROWS), :]
            loaded_ref[rows, :] = loaded_ref[rows, :] - correction
    second = jnp.dot(inv_ref[0], loaded_ref[...].astype(BF16), preferred_element_type=F32)
    out_ref[:MB, :] = second.astype(BF16)
    out_ref[MB:, :] = jnp.zeros((PIECE - MB, LANE), BF16)
    move.wait()
    for p in range(NPAN):
        owner = lax.rem(block_ref[p], cols) * doms + lax.div(block_ref[p], cols)
        out_ref[MB + 2 * p : MB + 2 * p + 2, :] = pair_ref[pl.ds(owner, 1)][0, 1]
        out_ref[MB + 4 + 2 * p : MB + 6 + 2 * p, :] = quad_ref[p]


def second_stage(got, loads, inverse, quads, panel_block):
    return pl.pallas_call(
        second_kernel,
        out_shape=jax.ShapeDtypeStruct((PIECE, LANE), BF16),
        in_specs=[VM] * 5 + [pl.BlockSpec(memory_space=pltpu.HBM)],
        out_specs=VM,
        scratch_shapes=[
            pltpu.SMEM(panel_block.shape, jnp.int32),
            pltpu.VMEM((2 * got.shape[0] * 2, LANE), F32),
            pltpu.VMEM(loads.shape[1:], F32),
            pltpu.SemaphoreType.DMA((1,)),
        ],
        compiler_params=PARAMS,
        name="second_stage",
    )(
        got.reshape(-1, LANE),
        got,
        loads,
        inverse,
        quads,
        pltpu.with_memory_space_constraint(panel_block, pltpu.HBM),
    )


def trace_kernel(
    gathered_ref, pair_ref, map_ref, block_hbm, shared_ref, last_ref, block_ref, second_ref, row_ref,
    tile_ref, sem
):
    move = pltpu.make_async_copy(block_hbm, block_ref, sem.at[0])
    move.start()
    cols = gathered_ref.shape[0]
    doms = map_ref.shape[1]
    core = lax.rem(lax.axis_index("col"), 2)
    for c in range(cols):
        second_ref[MB * c : MB * (c + 1), :] = gathered_ref[c, :MB, :]
        tile_ref[2 * c : 2 * c + 2, :] = pair_ref[c, pl.ds(MB // 2 + core, 1)][0].astype(F32)
    traces = jnp.dot(map_ref[0], second_ref[...], preferred_element_type=F32)
    tiles = [tile_ref[pl.ds(r, cols, stride=2), :] for r in range(2)]
    shared_ref[...] = jnp.concatenate(tiles, axis=0).astype(BF16)
    move.wait()
    quads = []
    for p in range(NPAN):
        lane = lax.rem(block_ref[p], cols)
        rows = gathered_ref[pl.ds(lane, 1)][0, MB : MB + 16, :].astype(F32)
        quads.append(rows[4 + 2 * p : 5 + 2 * p, :])
    tail = jnp.where(iota((1, LANE), 1) < 48, quads[0], pltpu.roll(quads[1], 48, 1))
    row_ref[pl.ds(0, doms, stride=2), :] = traces
    row_ref[pl.ds(1, doms, stride=2), :] = jnp.broadcast_to(tail, (doms, LANE))
    last_ref[...] = row_ref[...].astype(BF16)


def trace_stage(gathered, trace_map, panel_block):
    doms = trace_map.shape[1]
    return pl.pallas_call(
        trace_kernel,
        out_shape=(
            jax.ShapeDtypeStruct((16, LANE), BF16),
            jax.ShapeDtypeStruct((2 * doms, LANE), BF16),
        ),
        in_specs=[VM, VM, VM, pl.BlockSpec(memory_space=pltpu.HBM)],
        out_specs=(VM, VM),
        scratch_shapes=[
            pltpu.SMEM(panel_block.shape, jnp.int32),
            pltpu.VMEM((trace_map.shape[2], LANE), BF16),
            pltpu.VMEM((2 * doms, LANE), F32),
            pltpu.VMEM((16, LANE), F32),
            pltpu.SemaphoreType.DMA((1,)),
        ],
        compiler_params=PARAMS,
        name="trace_stage",
    )(gathered, gathered.reshape(-1, PIECE // 2, 2, LANE), trace_map, pltpu.with_memory_space_constraint(panel_block, pltpu.HBM))


def panel_of(block_ref, panel_ref, doms):
    for t in range(2 * doms):
        tile = block_ref[18 * (t // 2) + 8 * (t % 2) : 18 * (t // 2) + 8 * (t % 2) + 8, :]
        panel_ref[pl.ds(8 * (t // 16), 8), pl.ds(LANE * (t % 16), LANE)] = tile


def placed(low_ref, panel_ref, side):
    prior = lax.dot_general(
        low_ref[...], panel_ref[...], (((1,), (1,)), ((), ())), preferred_element_type=F32
    )
    both = jnp.concatenate([prior, prior], axis=1)
    return jnp.where((iota(both.shape, 1) >= P_SIZE) == (side == 1), both, 0.0)


def near_kernel(block_ref, low_ref, landing_ref, spots_ref, base_ref, panel_ref, row_ref):
    doms = landing_ref.shape[1]
    core = lax.rem(lax.axis_index("col"), 2)
    for h in range(doms):
        row_ref[2 * h : 2 * h + 2, :] = block_ref[18 * h + 16 : 18 * h + 18, :].astype(F32)
    traces = row_ref[pl.ds(0, doms, stride=2), :].astype(BF16)
    tails = row_ref[pl.ds(1, doms, stride=2), :]
    surface = jnp.dot(landing_ref[...], traces, preferred_element_type=F32)
    halves = []
    for p in range(NPAN):
        parts = []
        for t in range(3):
            pick = iota((16, LANE), 1) == iota((16, LANE), 0) + (48 * p + 16 * t)
            parts.append(turned(pick.astype(BF16), tails))
        halves.append((parts[2] + parts[1]) + parts[0])
    quads = jnp.concatenate(halves, axis=1)
    kernel_block = jnp.zeros_like(surface)
    for b in range(4):
        squared = jnp.zeros_like(surface)
        for c in range(3):
            shifted = spots_ref[:, c : c + 1] - quads[4 * c + b : 4 * c + b + 1, :]
            squared = squared + shifted * shifted
        green = jnp.cos(WAVE_NUMBER * jnp.sqrt(squared)) / (
            4.0 * math.pi * jnp.sqrt(squared + SMOOTHING * SMOOTHING)
        )
        kernel_block = kernel_block + quads[12 + b : 13 + b, :] * green
    panel_of(block_ref, panel_ref, doms)
    base_ref[...] = kernel_block - surface - placed(low_ref, panel_ref, core)


def far_kernel(block_ref, low_ref, base_ref, out_ref, panel_ref):
    core = lax.rem(lax.axis_index("col"), 2)
    panel_of(block_ref, panel_ref, block_ref.shape[0] // 18)
    out_ref[...] = base_ref[...] - placed(low_ref, panel_ref, 1 - core)


def near_stage(block, low, landing, spots):
    return pl.pallas_call(
        near_kernel,
        out_shape=jax.ShapeDtypeStruct((low.shape[0], LANE), F32),
        in_specs=[VM] * 4,
        out_specs=VM,
        scratch_shapes=[
            pltpu.VMEM(low.shape, BF16),
            pltpu.VMEM((2 * landing.shape[1], LANE), F32),
        ],
        compiler_params=PARAMS,
        cost_estimate=pl.CostEstimate(flops=40_000_000, bytes_accessed=1_000_000, transcendentals=100_000),
        name="near_stage",
    )(block, low, landing, spots)


def far_stage(block, low, base):
    return pl.pallas_call(
        far_kernel,
        out_shape=jax.ShapeDtypeStruct(base.shape, F32),
        in_specs=[VM] * 3,
        out_specs=VM,
        scratch_shapes=[pltpu.VMEM(low.shape, BF16)],
        compiler_params=PARAMS,
        name="far_stage",
    )(block, low, base)


def local(
    inverse,
    trace_map,
    panel_coupling,
    coupling,
    neighbours,
    iface_count,
    surface_rows,
    factor,
    colloc,
    quad_points,
    quad_weight,
    panel_block,
):
    doms = lax.axis_size("dom")
    cols = lax.axis_size("col")
    sent, inverse, trace_map, loads, factor_low, landing, spots = first_stage(
        inverse, trace_map, panel_coupling, coupling, neighbours, iface_count, surface_rows, factor,
        colloc, quad_points, quad_weight, doms,
    )
    got = lax.all_to_all(sent.reshape(doms, ROWS // 2, 2, LANE), "dom", 0, 0, tiled=True)
    sent, quads = mix_stage(got, factor_low, panel_block, doms, cols)

    sent = sent.reshape(cols * doms, 2, 2, LANE)
    got = lax.all_to_all(sent, ("col", "dom"), 0, 0, tiled=True)
    pieces = second_stage(got, loads, inverse, quads, panel_block)
    gathered = lax.all_gather(pieces, "col", axis=0, tiled=False)
    shared, last = trace_stage(gathered, trace_map, panel_block)

    sent = jnp.concatenate(
        [
            jnp.broadcast_to(shared.reshape(1, 8, 2, LANE), (doms, 8, 2, LANE)),
            last.reshape(doms, 1, 2, LANE),
        ],
        axis=1,
    )
    got = lax.all_to_all(sent, "dom", 0, 0, tiled=True)
    other = lax.ppermute(got, "col", [(c, c ^ 1) for c in range(cols)])
    base = near_stage(got.reshape(18 * doms, LANE), factor_low, landing, spots)
    return far_stage(other.reshape(18 * doms, LANE), factor_low, base)


def solution(mesh):
    in_specs = (
        P("dom", "col", None),
        P("dom", "col", None),
        P("dom", None, None),
        P("dom", None, "col"),
        P("dom", None),
        P(),
        P("dom", "col", None, None),
        P(("dom", "col"), None),
        P(None, ("dom", "col")),
        P(None, None, ("dom", "col")),
        P(None, ("dom", "col")),
        P(),
    )
    out_specs = P(("dom", "col"), None)
    return jax.shard_map(local, mesh=mesh, in_specs=in_specs, out_specs=out_specs, check_vma=False)
```

```python
import math

import jax
import jax.numpy as jnp
from jax import lax
from jax.experimental import pallas as pl
from jax.experimental.pallas import tpu as pltpu
from jax.sharding import Mesh
from jax.sharding import PartitionSpec as P

MB = 208
P_SIZE = 64
NPAN = 2
LIVE = 128
MAX_LIVE = 112
LANE = 128
ROWS = 20

WAVE_NUMBER = 8.0
SMOOTHING = 0.05

F32 = jnp.float32
BF16 = jnp.bfloat16
VM = pl.BlockSpec(memory_space=pltpu.VMEM)
PARAMS = pltpu.CompilerParams(vmem_limit_bytes=16 * 1024 * 1024)


def iota(shape, axis):
    return lax.broadcasted_iota(jnp.int32, shape, axis)


def terms(values):
    high = values.astype(BF16).astype(F32)
    rest = values - high
    middle = rest.astype(BF16).astype(F32)
    return high, middle, rest - middle


def turned(left, right):
    return lax.dot_general(
        left, right.astype(BF16), (((1,), (1,)), ((), ())), preferred_element_type=F32
    )


def first_kernel(
    inv_hbm, map_hbm, loads_hbm, coup_hbm, listed_hbm, count_hbm, rows_hbm, factor_hbm, colloc_hbm,
    points_hbm, weight_hbm,
    sent_ref, inv_ref, map_ref, loads_ref, low_ref, landing_ref, spots_ref,
    coup_in, listed_ref, count_ref, rows_ref, factor_ref, colloc_ref, points_ref, weight_ref,
    quad_ref, coup_scr, spot_scr, first_ref, row_ref, sems,
):
    doms = landing_ref.shape[1]
    moves = [
        pltpu.make_async_copy(src, dst, sems.at[i])
        for i, (src, dst) in enumerate(
            [
                (listed_hbm, listed_ref),
                (count_hbm, count_ref),
                (points_hbm, points_ref),
                (weight_hbm, weight_ref),
                (coup_hbm, coup_in),
                (rows_hbm, rows_ref),
                (colloc_hbm, colloc_ref),
                (factor_hbm, factor_ref),
                (loads_hbm, loads_ref),
                (inv_hbm, inv_ref),
                (map_hbm, map_ref),
            ]
        )
    ]
    for move in moves:
        move.start()
    coup_scr[...] = jnp.zeros_like(coup_scr)
    row_ref[...] = jnp.zeros_like(row_ref)
    spot_scr[...] = jnp.zeros_like(spot_scr)
    for move in moves[:7]:
        move.wait()
    count = count_ref[lax.axis_index("dom")]
    for c in range(3):
        quad_ref[4 * c : 4 * c + 4, :] = points_ref[c]
    quad_ref[12:16, :] = weight_ref[...]
    for k in range(6):
        coup_scr[k : k + 1, :] = coup_in[k][:, :LIVE]
    spot_scr[0:3, :] = colloc_ref[...]
    quads = jnp.concatenate(list(terms(quad_ref[...])) + [jnp.zeros((80, doms), F32)], axis=0)
    weights = list(terms(coup_scr[...]))
    even = jnp.concatenate([jnp.zeros((48, LIVE), F32)] + weights + [jnp.zeros((56, LIVE), F32)], axis=0)
    odd = jnp.concatenate([jnp.zeros((72, LIVE), F32)] + weights + [jnp.zeros((32, LIVE), F32)], axis=0)
    spots = jnp.concatenate(list(terms(spot_scr[...])) + [jnp.zeros((104, doms), F32)], axis=0)
    at = iota((doms, LIVE), 1)
    pair = 2 * iota((doms, LIVE), 0)
    unit = (iota((doms, doms), 0) == iota((doms, doms), 1)).astype(BF16)
    misc = turned(unit, quads)
    misc = misc + turned((at == pair).astype(BF16), even)
    misc = misc + turned((at == pair + 1).astype(BF16), odd)
    for k in range(6):
        misc = jnp.where(at == 96 + k, listed_ref[0, k].astype(F32), misc)
    misc = jnp.where(at == 102, count.astype(F32), misc)
    row_ref[pl.ds(2, doms, stride=4), :] = misc
    spots = turned(unit, spots)
    spots_ref[...] = spots + pltpu.roll(spots, LANE - 8, 1) + pltpu.roll(spots, LANE - 16, 1)
    landing_ref[...] = (iota((doms, doms), 0) == rows_ref[0, 0]).astype(BF16)
    moves[7].wait()
    for h in range(doms):
        tile = factor_ref[pl.ds(16 * (h // 16), 16), pl.ds(LANE * (h % 16), LANE)]
        sent_ref[ROWS * h : ROWS * h + 16, :] = tile.astype(BF16)
    low_ref[...] = factor_ref[...].astype(BF16)
    for move in moves[8:10]:
        move.wait()
    first = jnp.dot(inv_ref[0, :LIVE, :], loads_ref[0], preferred_element_type=F32)
    first_ref[...] = jnp.where(iota((LIVE, LANE), 0) < count, first, 0.0)
    row_ref[pl.ds(0, doms, stride=4), :] = first_ref[pl.ds(0, doms, stride=2), :]
    row_ref[pl.ds(1, doms, stride=4), :] = first_ref[pl.ds(1, doms, stride=2), :]
    for h in range(doms):
        sent_ref[ROWS * h + 16 : ROWS * h + 20, :] = row_ref[4 * h : 4 * h + 4, :].astype(BF16)
    moves[10].wait()


def first_stage(
    inverse, trace_map, panel_coupling, coupling, neighbours, iface_count, surface_rows, factor,
    colloc, quad_points, quad_weight, doms,
):
    shape = jax.ShapeDtypeStruct
    coupling = coupling.transpose(1, 0, 2)
    return pl.pallas_call(
        first_kernel,
        out_shape=(
            shape((ROWS * doms, LANE), BF16),
            shape(inverse.shape, BF16),
            shape(trace_map.shape, BF16),
            shape(panel_coupling.shape, BF16),
            shape(factor.shape, BF16),
            shape((doms, doms), BF16),
            shape((doms, LANE), F32),
        ),
        in_specs=[pl.BlockSpec(memory_space=pltpu.HBM)] * 11,
        out_specs=(VM,) * 7,
        scratch_shapes=[
            pltpu.VMEM(coupling.shape, F32),
            pltpu.SMEM(neighbours.shape, jnp.int32),
            pltpu.SMEM(iface_count.shape, jnp.int32),
            pltpu.VMEM(surface_rows.shape, jnp.int32),
            pltpu.VMEM(factor.shape, F32),
            pltpu.VMEM(colloc.shape, F32),
            pltpu.VMEM(quad_points.shape, F32),
            pltpu.VMEM(quad_weight.shape, F32),
            pltpu.VMEM((16, doms), F32),
            pltpu.VMEM((8, LIVE), F32),
            pltpu.VMEM((8, doms), F32),
            pltpu.VMEM((LIVE, LANE), F32),
            pltpu.VMEM((4 * doms, LANE), F32),
            pltpu.SemaphoreType.DMA((11,)),
        ],
        compiler_params=PARAMS,
        name="first_stage",
    )(
        *(
            pltpu.with_memory_space_constraint(x, pltpu.HBM)
            for x in (
                inverse, trace_map, panel_coupling, coupling, neighbours, iface_count, surface_rows,
                factor, colloc, quad_points, quad_weight,
            )
        )
    )


def mix_kernel(got_ref, pair_ref, block_hbm, sent_ref, picks_ref, block_ref, row_ref, sem):
    doms = pair_ref.shape[0]
    copies = sent_ref.shape[0]
    cols = 2 * copies
    move = pltpu.make_async_copy(block_hbm, block_ref, sem.at[0])
    move.start()
    for h in range(doms):
        row_ref[4 * h : 4 * h + 4, :] = got_ref[ROWS * h + 16 : ROWS * h + 20, :].astype(F32)
    misc = row_ref[pl.ds(2, doms, stride=4), :]
    weights = misc + pltpu.roll(misc, LANE - 8, 1) + pltpu.roll(misc, LANE - 16, 1)
    sources = iota((doms, doms), 1).astype(F32)
    mixed = []
    for r in range(2):
        mixing = jnp.zeros((doms, doms), F32)
        for k in range(6):
            lane = 48 + 24 * r + k
            mixing = mixing + jnp.where(
                misc[:, 96 + k : 97 + k] == sources, weights[:, lane : lane + 1], 0.0
            )
        summed = jnp.dot(
            mixing,
            row_ref[pl.ds(r, doms, stride=4), :],
            precision=lax.Precision.HIGHEST,
            preferred_element_type=F32,
        )
        row = (2 * lax.axis_index("dom") + r).astype(F32)
        mixed.append(jnp.where(misc[:, 102:103] > row, summed, 0.0))
    row_ref[pl.ds(0, doms, stride=2), :] = mixed[0]
    row_ref[pl.ds(1, doms, stride=2), :] = mixed[1]
    correction = row_ref[: 2 * doms, :].astype(BF16)
    for z in range(copies):
        sent_ref[z] = correction
    move.wait()
    for p in range(NPAN):
        owner = lax.div(block_ref[p], cols)
        picks_ref[p] = pair_ref[pl.ds(owner, 1)][0]


def mix_stage(got, panel_block, doms, copies):
    return pl.pallas_call(
        mix_kernel,
        out_shape=(
            jax.ShapeDtypeStruct((copies, 2 * doms, LANE), BF16),
            jax.ShapeDtypeStruct((NPAN, ROWS // 2, 2, LANE), BF16),
        ),
        in_specs=[VM, VM, pl.BlockSpec(memory_space=pltpu.HBM)],
        out_specs=(VM, VM),
        scratch_shapes=[
            pltpu.SMEM(panel_block.shape, jnp.int32),
            pltpu.VMEM((4 * doms, LANE), F32),
            pltpu.SemaphoreType.DMA((1,)),
        ],
        compiler_params=PARAMS,
        name="mix_stage",
    )(
        got.reshape(ROWS * doms, LANE),
        got,
        pltpu.with_memory_space_constraint(panel_block, pltpu.HBM),
    )


def second_kernel(own_ref, other_ref, loads_ref, inv_ref, picks_ref, out_ref, loaded_ref):
    first_core = lax.axis_index("core") == 0
    for c in range(2 * own_ref.shape[0]):
        own = own_ref[c // 2, :MAX_LIVE, :].astype(F32)
        other = other_ref[c // 2, :MAX_LIVE, :].astype(F32)
        correction = jnp.where(first_core == (c % 2 == 0), own, other)
        top = loads_ref[0, MB * c : MB * c + MAX_LIVE, :].astype(F32) - correction
        loaded_ref[MB * c : MB * c + MAX_LIVE, :] = top.astype(BF16)
        loaded_ref[MB * c + MAX_LIVE : MB * (c + 1), :] = loads_ref[0, MB * c + MAX_LIVE : MB * (c + 1), :]
    second = jnp.dot(inv_ref[0], loaded_ref[...], preferred_element_type=F32)
    out_ref[:MB, :] = second.astype(BF16)
    out_ref[MB + 32 :, :] = jnp.zeros((16, LANE), BF16)
    for p in range(NPAN):
        out_ref[MB + 16 * p : MB + 16 * p + 16, :] = picks_ref[ROWS * p : ROWS * p + 16, :]
        out_ref[MB + 32 + 2 * p : MB + 34 + 2 * p, :] = picks_ref[ROWS * p + 18 : ROWS * p + 20, :]


def second_stage(own, other, loads, inverse, picks):
    return pl.pallas_call(
        second_kernel,
        out_shape=jax.ShapeDtypeStruct((MB + 48, LANE), BF16),
        in_specs=[VM] * 5,
        out_specs=VM,
        scratch_shapes=[pltpu.VMEM(loads.shape[1:], BF16)],
        compiler_params=PARAMS,
        name="second_stage",
    )(own, other, loads, inverse, picks.reshape(NPAN * ROWS, LANE))


def trace_kernel(
    gathered_ref, map_ref, block_hbm, shared_ref, last_ref, block_ref, second_ref, row_ref, sem
):
    move = pltpu.make_async_copy(block_hbm, block_ref, sem.at[0])
    move.start()
    cols = gathered_ref.shape[0]
    doms = map_ref.shape[1]
    core = lax.axis_index("core")
    for c in range(cols):
        second_ref[MB * c : MB * (c + 1), :] = gathered_ref[c, :MB, :]
    traces = jnp.dot(map_ref[0], second_ref[...], preferred_element_type=F32)
    move.wait()
    lanes = [lax.rem(block_ref[p], cols) for p in range(NPAN)]
    own = jnp.where(core == 0, lanes[0], lanes[1])
    first = gathered_ref[pl.ds(own, 1)][0, MB : MB + 16, :]
    second = gathered_ref[pl.ds(own, 1)][0, MB + 16 : MB + 32, :]
    shared_ref[...] = jnp.where(core == 0, first.astype(F32), second.astype(F32)).astype(BF16)
    quads = [
        gathered_ref[pl.ds(lanes[p], 1)][0, MB + 32 : MB + 48, :].astype(F32)[2 * p : 2 * p + 1, :]
        for p in range(NPAN)
    ]
    tail = jnp.where(iota((1, LANE), 1) < 48, quads[0], pltpu.roll(quads[1], 48, 1))
    row_ref[pl.ds(0, doms, stride=2), :] = traces
    row_ref[pl.ds(1, doms, stride=2), :] = jnp.broadcast_to(tail, (doms, LANE))
    last_ref[...] = row_ref[...].astype(BF16)


def trace_stage(gathered, trace_map, panel_block):
    doms = trace_map.shape[1]
    return pl.pallas_call(
        trace_kernel,
        out_shape=(
            jax.ShapeDtypeStruct((16, LANE), BF16),
            jax.ShapeDtypeStruct((2 * doms, LANE), BF16),
        ),
        in_specs=[VM, VM, pl.BlockSpec(memory_space=pltpu.HBM)],
        out_specs=(VM, VM),
        scratch_shapes=[
            pltpu.SMEM(panel_block.shape, jnp.int32),
            pltpu.VMEM((trace_map.shape[2], LANE), BF16),
            pltpu.VMEM((2 * doms, LANE), F32),
            pltpu.SemaphoreType.DMA((1,)),
        ],
        compiler_params=PARAMS,
        name="trace_stage",
    )(gathered, trace_map, pltpu.with_memory_space_constraint(panel_block, pltpu.HBM))


def panel_of(block_ref, panel_ref, doms):
    for h in range(doms):
        tile = block_ref[18 * h : 18 * h + 16, :]
        panel_ref[pl.ds(16 * (h // 16), 16), pl.ds(LANE * (h % 16), LANE)] = tile


def placed(low_ref, panel_ref, side):
    prior = lax.dot_general(
        low_ref[...], panel_ref[...], (((1,), (1,)), ((), ())), preferred_element_type=F32
    )
    both = jnp.concatenate([prior, prior], axis=1)
    return jnp.where((iota(both.shape, 1) >= P_SIZE) == (side == 1), both, 0.0)


def near_kernel(block_ref, low_ref, landing_ref, spots_ref, base_ref, panel_ref, row_ref):
    doms = landing_ref.shape[1]
    core = lax.axis_index("core")
    for h in range(doms):
        row_ref[2 * h : 2 * h + 2, :] = block_ref[18 * h + 16 : 18 * h + 18, :].astype(F32)
    traces = row_ref[pl.ds(0, doms, stride=2), :].astype(BF16)
    tails = row_ref[pl.ds(1, doms, stride=2), :]
    surface = jnp.dot(landing_ref[...], traces, preferred_element_type=F32)
    halves = []
    for p in range(NPAN):
        parts = []
        for t in range(3):
            pick = iota((16, LANE), 1) == iota((16, LANE), 0) + (48 * p + 16 * t)
            parts.append(turned(pick.astype(BF16), tails))
        halves.append((parts[2] + parts[1]) + parts[0])
    quads = jnp.concatenate(halves, axis=1)
    kernel_block = jnp.zeros_like(surface)
    for b in range(4):
        squared = jnp.zeros_like(surface)
        for c in range(3):
            shifted = spots_ref[:, c : c + 1] - quads[4 * c + b : 4 * c + b + 1, :]
            squared = squared + shifted * shifted
        green = jnp.cos(WAVE_NUMBER * jnp.sqrt(squared)) / (
            4.0 * math.pi * jnp.sqrt(squared + SMOOTHING * SMOOTHING)
        )
        kernel_block = kernel_block + quads[12 + b : 13 + b, :] * green
    panel_of(block_ref, panel_ref, doms)
    base_ref[...] = kernel_block - surface - placed(low_ref, panel_ref, core)


def far_kernel(block_ref, low_ref, base_ref, out_ref, panel_ref):
    core = lax.axis_index("core")
    panel_of(block_ref, panel_ref, block_ref.shape[0] // 18)
    out_ref[...] = base_ref[...] - placed(low_ref, panel_ref, 1 - core)


def near_stage(block, low, landing, spots):
    return pl.pallas_call(
        near_kernel,
        out_shape=jax.ShapeDtypeStruct((low.shape[0], LANE), F32),
        in_specs=[VM] * 4,
        out_specs=VM,
        scratch_shapes=[
            pltpu.VMEM(low.shape, BF16),
            pltpu.VMEM((2 * landing.shape[1], LANE), F32),
        ],
        compiler_params=PARAMS,
        cost_estimate=pl.CostEstimate(flops=40_000_000, bytes_accessed=1_000_000, transcendentals=100_000),
        name="near_stage",
    )(block, low, landing, spots)


def far_stage(block, low, base):
    return pl.pallas_call(
        far_kernel,
        out_shape=jax.ShapeDtypeStruct(base.shape, F32),
        in_specs=[VM] * 3,
        out_specs=VM,
        scratch_shapes=[pltpu.VMEM(low.shape, BF16)],
        compiler_params=PARAMS,
        name="far_stage",
    )(block, low, base)


def local(
    inverse,
    trace_map,
    panel_coupling,
    coupling,
    neighbours,
    iface_count,
    surface_rows,
    factor,
    colloc,
    quad_points,
    quad_weight,
    panel_block,
):
    doms = lax.axis_size("dom")
    levels = lax.axis_size("zh")
    sent, inverse, trace_map, loads, factor_low, landing, spots = first_stage(
        inverse, trace_map, panel_coupling, coupling, neighbours, iface_count, surface_rows, factor,
        colloc, quad_points, quad_weight, doms,
    )
    got = lax.all_to_all(sent.reshape(doms, ROWS // 2, 2, LANE), "dom", 0, 0, tiled=True)
    sent, picks = mix_stage(got, panel_block, doms, levels)

    sent = sent.reshape(levels * doms, 2, LANE)
    own = lax.all_to_all(sent, ("zh", "dom"), 0, 0, tiled=True)
    own = own.reshape(levels, 2 * doms, LANE)
    other = lax.ppermute(own, "core", [(0, 1), (1, 0)])
    pieces = second_stage(own, other, loads, inverse, picks)
    gathered = lax.all_gather(pieces, ("zh", "core"), axis=0, tiled=False)
    shared, last = trace_stage(gathered, trace_map, panel_block)

    sent = jnp.concatenate(
        [
            jnp.broadcast_to(shared.reshape(1, 8, 2, LANE), (doms, 8, 2, LANE)),
            last.reshape(doms, 1, 2, LANE),
        ],
        axis=1,
    )
    got = lax.all_to_all(sent, "dom", 0, 0, tiled=True)
    other = lax.ppermute(got, "core", [(0, 1), (1, 0)])
    base = near_stage(got.reshape(18 * doms, LANE), factor_low, landing, spots)
    return far_stage(other.reshape(18 * doms, LANE), factor_low, base)


def solution(mesh):
    split = Mesh(mesh.devices.reshape(mesh.shape["dom"], -1, 2), ("dom", "zh", "core"))
    col = ("zh", "core")
    rows = ("dom", "zh", "core")
    in_specs = (
        P("dom", col, None),
        P("dom", col, None),
        P("dom", None, None),
        P("dom", None, col),
        P("dom", None),
        P(),
        P("dom", col, None, None),
        P(rows, None),
        P(None, rows),
        P(None, None, rows),
        P(None, rows),
        P(),
    )
    out_specs = P(rows, None)
    return jax.shard_map(local, mesh=split, in_specs=in_specs, out_specs=out_specs, check_vma=False)
```

```python
import math

import jax
import jax.numpy as jnp
from jax import lax
from jax.experimental import pallas as pl
from jax.experimental.pallas import tpu as pltpu
from jax.sharding import PartitionSpec as P

MB = 208
P_SIZE = 64
NPAN = 2
LIVE = 128
MAX_LIVE = 112
LANE = 128
ROWS = 20

WAVE_NUMBER = 8.0
SMOOTHING = 0.05

F32 = jnp.float32
BF16 = jnp.bfloat16
VM = pl.BlockSpec(memory_space=pltpu.VMEM)
PARAMS = pltpu.CompilerParams(vmem_limit_bytes=16 * 1024 * 1024)


def iota(shape, axis):
    return lax.broadcasted_iota(jnp.int32, shape, axis)


def terms(values):
    high = values.astype(BF16).astype(F32)
    rest = values - high
    middle = rest.astype(BF16).astype(F32)
    return high, middle, rest - middle


def turned(left, right):
    return lax.dot_general(
        left, right.astype(BF16), (((1,), (1,)), ((), ())), preferred_element_type=F32
    )


def first_kernel(
    inv_hbm, map_hbm, loads_hbm, coup_hbm, listed_hbm, count_hbm, rows_hbm, factor_hbm, colloc_hbm,
    points_hbm, weight_hbm,
    sent_ref, inv_ref, map_ref, loads_ref, low_ref, landing_ref, spots_ref,
    coup_in, listed_ref, count_ref, rows_ref, factor_ref, colloc_ref, points_ref, weight_ref,
    quad_ref, coup_scr, spot_scr, first_ref, row_ref, sems,
):
    doms = landing_ref.shape[1]
    moves = [
        pltpu.make_async_copy(src, dst, sems.at[i])
        for i, (src, dst) in enumerate(
            [
                (listed_hbm, listed_ref),
                (count_hbm, count_ref),
                (points_hbm, points_ref),
                (weight_hbm, weight_ref),
                (coup_hbm, coup_in),
                (rows_hbm, rows_ref),
                (colloc_hbm, colloc_ref),
                (loads_hbm, loads_ref),
                (inv_hbm.at[:, :LIVE], inv_ref.at[:, :LIVE]),
                (factor_hbm, factor_ref),
                (inv_hbm.at[:, LIVE:], inv_ref.at[:, LIVE:]),
                (map_hbm, map_ref),
            ]
        )
    ]
    for move in moves:
        move.start()
    coup_scr[...] = jnp.zeros_like(coup_scr)
    row_ref[...] = jnp.zeros_like(row_ref)
    spot_scr[...] = jnp.zeros_like(spot_scr)
    for move in moves[:7]:
        move.wait()
    count = count_ref[lax.axis_index("dom")]
    for c in range(3):
        quad_ref[4 * c : 4 * c + 4, :] = points_ref[c]
    quad_ref[12:16, :] = weight_ref[...]
    for k in range(6):
        coup_scr[k : k + 1, :] = coup_in[k][:, :LIVE]
    spot_scr[0:3, :] = colloc_ref[...]
    quads = jnp.concatenate(list(terms(quad_ref[...])) + [jnp.zeros((80, doms), F32)], axis=0)
    weights = list(terms(coup_scr[...]))
    even = jnp.concatenate([jnp.zeros((48, LIVE), F32)] + weights + [jnp.zeros((56, LIVE), F32)], axis=0)
    odd = jnp.concatenate([jnp.zeros((72, LIVE), F32)] + weights + [jnp.zeros((32, LIVE), F32)], axis=0)
    spots = jnp.concatenate(list(terms(spot_scr[...])) + [jnp.zeros((104, doms), F32)], axis=0)
    at = iota((doms, LIVE), 1)
    pair = 2 * iota((doms, LIVE), 0)
    unit = (iota((doms, doms), 0) == iota((doms, doms), 1)).astype(BF16)
    misc = turned(unit, quads)
    misc = misc + turned((at == pair).astype(BF16), even)
    misc = misc + turned((at == pair + 1).astype(BF16), odd)
    for k in range(6):
        misc = jnp.where(at == 96 + k, listed_ref[0, k].astype(F32), misc)
    misc = jnp.where(at == 102, count.astype(F32), misc)
    row_ref[pl.ds(2, doms, stride=4), :] = misc
    spots = turned(unit, spots)
    spots_ref[...] = spots + pltpu.roll(spots, LANE - 8, 1) + pltpu.roll(spots, LANE - 16, 1)
    landing_ref[...] = (iota((doms, doms), 0) == rows_ref[0, 0]).astype(BF16)
    for move in moves[7:9]:
        move.wait()
    first = jnp.dot(inv_ref[0, :LIVE, :], loads_ref[0], preferred_element_type=F32)
    first_ref[...] = jnp.where(iota((LIVE, LANE), 0) < count, first, 0.0)
    row_ref[pl.ds(0, doms, stride=4), :] = first_ref[pl.ds(0, doms, stride=2), :]
    row_ref[pl.ds(1, doms, stride=4), :] = first_ref[pl.ds(1, doms, stride=2), :]
    for h in range(doms):
        sent_ref[ROWS * h + 16 : ROWS * h + 20, :] = row_ref[4 * h : 4 * h + 4, :].astype(BF16)
    moves[9].wait()
    for h in range(doms):
        tile = factor_ref[pl.ds(16 * (h // 16), 16), pl.ds(LANE * (h % 16), LANE)]
        sent_ref[ROWS * h : ROWS * h + 16, :] = tile.astype(BF16)
    low_ref[...] = factor_ref[...].astype(BF16)
    for move in moves[10:]:
        move.wait()


def first_stage(
    inverse, trace_map, panel_coupling, coupling, neighbours, iface_count, surface_rows, factor,
    colloc, quad_points, quad_weight, doms,
):
    shape = jax.ShapeDtypeStruct
    coupling = coupling.transpose(1, 0, 2)
    return pl.pallas_call(
        first_kernel,
        out_shape=(
            shape((ROWS * doms, LANE), BF16),
            shape(inverse.shape, BF16),
            shape(trace_map.shape, BF16),
            shape(panel_coupling.shape, BF16),
            shape(factor.shape, BF16),
            shape((doms, doms), BF16),
            shape((doms, LANE), F32),
        ),
        in_specs=[pl.BlockSpec(memory_space=pltpu.HBM)] * 11,
        out_specs=(VM,) * 7,
        scratch_shapes=[
            pltpu.VMEM(coupling.shape, F32),
            pltpu.SMEM(neighbours.shape, jnp.int32),
            pltpu.SMEM(iface_count.shape, jnp.int32),
            pltpu.VMEM(surface_rows.shape, jnp.int32),
            pltpu.VMEM(factor.shape, F32),
            pltpu.VMEM(colloc.shape, F32),
            pltpu.VMEM(quad_points.shape, F32),
            pltpu.VMEM(quad_weight.shape, F32),
            pltpu.VMEM((16, doms), F32),
            pltpu.VMEM((8, LIVE), F32),
            pltpu.VMEM((8, doms), F32),
            pltpu.VMEM((LIVE, LANE), F32),
            pltpu.VMEM((4 * doms, LANE), F32),
            pltpu.SemaphoreType.DMA((12,)),
        ],
        compiler_params=PARAMS,
        name="first_stage",
    )(
        *(
            pltpu.with_memory_space_constraint(x, pltpu.HBM)
            for x in (
                inverse, trace_map, panel_coupling, coupling, neighbours, iface_count, surface_rows,
                factor, colloc, quad_points, quad_weight,
            )
        )
    )


def mix_kernel(got_ref, pair_ref, block_hbm, sent_ref, picks_ref, lane_ref, block_ref, row_ref, sem):
    doms = pair_ref.shape[0]
    cols = sent_ref.shape[0]
    move = pltpu.make_async_copy(block_hbm, block_ref, sem.at[0])
    move.start()
    for h in range(doms):
        row_ref[4 * h : 4 * h + 4, :] = got_ref[ROWS * h + 16 : ROWS * h + 20, :].astype(F32)
    misc = row_ref[pl.ds(2, doms, stride=4), :]
    weights = misc + pltpu.roll(misc, LANE - 8, 1) + pltpu.roll(misc, LANE - 16, 1)
    sources = iota((doms, doms), 1).astype(F32)
    mixed = []
    for r in range(2):
        mixing = jnp.zeros((doms, doms), F32)
        for k in range(6):
            lane = 48 + 24 * r + k
            mixing = mixing + jnp.where(
                misc[:, 96 + k : 97 + k] == sources, weights[:, lane : lane + 1], 0.0
            )
        summed = jnp.dot(
            mixing,
            row_ref[pl.ds(r, doms, stride=4), :],
            precision=lax.Precision.HIGHEST,
            preferred_element_type=F32,
        )
        row = (2 * lax.axis_index("dom") + r).astype(F32)
        mixed.append(jnp.where(misc[:, 102:103] > row, summed, 0.0))
    row_ref[pl.ds(0, doms, stride=2), :] = mixed[0]
    row_ref[pl.ds(1, doms, stride=2), :] = mixed[1]
    correction = row_ref[: 2 * doms, :].astype(BF16)
    for c in range(cols):
        sent_ref[c] = correction
    move.wait()
    for p in range(NPAN):
        owner = lax.div(block_ref[p], cols)
        picks_ref[p] = pair_ref[pl.ds(owner, 1)][0]
        lane_ref[p] = jnp.full((8, LANE), lax.rem(block_ref[p], cols), jnp.int32)


def mix_stage(got, panel_block, doms, cols):
    return pl.pallas_call(
        mix_kernel,
        out_shape=(
            jax.ShapeDtypeStruct((cols, 2 * doms, LANE), BF16),
            jax.ShapeDtypeStruct((NPAN, ROWS // 2, 2, LANE), BF16),
            jax.ShapeDtypeStruct((NPAN, 8, LANE), jnp.int32),
        ),
        in_specs=[VM, VM, pl.BlockSpec(memory_space=pltpu.HBM)],
        out_specs=(VM, VM, VM),
        scratch_shapes=[
            pltpu.SMEM(panel_block.shape, jnp.int32),
            pltpu.VMEM((4 * doms, LANE), F32),
            pltpu.SemaphoreType.DMA((1,)),
        ],
        compiler_params=PARAMS,
        name="mix_stage",
    )(
        got.reshape(ROWS * doms, LANE),
        got,
        pltpu.with_memory_space_constraint(panel_block, pltpu.HBM),
    )


def second_kernel(correction_ref, loads_ref, inv_ref, picks_ref, out_ref, loaded_ref):
    cols = correction_ref.shape[0]
    for c in range(cols):
        top = loads_ref[0, MB * c : MB * c + MAX_LIVE, :].astype(F32)
        top = top - correction_ref[c, :MAX_LIVE, :].astype(F32)
        loaded_ref[MB * c : MB * c + MAX_LIVE, :] = top.astype(BF16)
        loaded_ref[MB * c + MAX_LIVE : MB * (c + 1), :] = loads_ref[0, MB * c + MAX_LIVE : MB * (c + 1), :]
    second = jnp.dot(inv_ref[0], loaded_ref[...], preferred_element_type=F32)
    out_ref[:MB, :] = second.astype(BF16)
    out_ref[MB + 32 :, :] = jnp.zeros((16, LANE), BF16)
    for p in range(NPAN):
        out_ref[MB + 16 * p : MB + 16 * p + 16, :] = picks_ref[ROWS * p : ROWS * p + 16, :]
        out_ref[MB + 32 + 2 * p : MB + 34 + 2 * p, :] = picks_ref[ROWS * p + 18 : ROWS * p + 20, :]


def second_stage(correction, loads, inverse, picks):
    return pl.pallas_call(
        second_kernel,
        out_shape=jax.ShapeDtypeStruct((MB + 48, LANE), BF16),
        in_specs=[VM] * 4,
        out_specs=VM,
        scratch_shapes=[pltpu.VMEM(loads.shape[1:], BF16)],
        compiler_params=PARAMS,
        name="second_stage",
    )(correction, loads, inverse, picks.reshape(NPAN * ROWS, LANE))


def trace_kernel(gathered_ref, map_ref, lane_ref, sent_ref, second_ref, row_ref):
    cols = gathered_ref.shape[0]
    doms = map_ref.shape[1]
    first_core = lax.rem(lax.axis_index("col"), 2) == 0
    lanes = [lane_ref[p][:1, :] for p in range(NPAN)]
    chunk = jnp.zeros((16, LANE), F32)
    quads = [jnp.zeros((1, LANE), F32)] * NPAN
    for c in range(cols):
        second_ref[MB * c : MB * (c + 1), :] = gathered_ref[c, :MB, :]
        rest = gathered_ref[c, MB : MB + 48, :].astype(F32)
        tile = jnp.where(first_core, rest[:16], rest[16:32])
        chunk = jnp.where(jnp.where(first_core, lanes[0], lanes[1]) == c, tile, chunk)
        for p in range(NPAN):
            quads[p] = jnp.where(lanes[p] == c, rest[32 + 2 * p : 33 + 2 * p], quads[p])
    tail = jnp.where(iota((1, LANE), 1) < 48, quads[0], pltpu.roll(quads[1], 48, 1))
    row_ref[pl.ds(1, doms, stride=2), :] = jnp.broadcast_to(tail, (doms, LANE))
    row_ref[pl.ds(0, doms, stride=2), :] = jnp.dot(
        map_ref[0], second_ref[...], preferred_element_type=F32
    )
    chunk = chunk.astype(BF16)
    for h in range(doms):
        sent_ref[18 * h : 18 * h + 16, :] = chunk
        sent_ref[18 * h + 16 : 18 * h + 18, :] = row_ref[2 * h : 2 * h + 2, :].astype(BF16)


def trace_stage(gathered, trace_map, lanes):
    doms = trace_map.shape[1]
    return pl.pallas_call(
        trace_kernel,
        out_shape=jax.ShapeDtypeStruct((18 * doms, LANE), BF16),
        in_specs=[VM, VM, VM],
        out_specs=VM,
        scratch_shapes=[
            pltpu.VMEM((trace_map.shape[2], LANE), BF16),
            pltpu.VMEM((2 * doms, LANE), F32),
        ],
        compiler_params=PARAMS,
        name="trace_stage",
    )(gathered, trace_map, lanes)


def panel_of(block_ref, panel_ref, doms):
    for h in range(doms):
        tile = block_ref[18 * h : 18 * h + 16, :]
        panel_ref[pl.ds(16 * (h // 16), 16), pl.ds(LANE * (h % 16), LANE)] = tile


def placed(low_ref, panel_ref, side):
    prior = lax.dot_general(
        low_ref[...], panel_ref[...], (((1,), (1,)), ((), ())), preferred_element_type=F32
    )
    both = jnp.concatenate([prior, prior], axis=1)
    return jnp.where((iota(both.shape, 1) >= P_SIZE) == (side == 1), both, 0.0)


def near_kernel(block_ref, low_ref, landing_ref, spots_ref, base_ref, panel_ref, row_ref):
    doms = landing_ref.shape[1]
    core = lax.rem(lax.axis_index("col"), 2)
    for h in range(doms):
        row_ref[2 * h : 2 * h + 2, :] = block_ref[18 * h + 16 : 18 * h + 18, :].astype(F32)
    traces = row_ref[pl.ds(0, doms, stride=2), :].astype(BF16)
    tails = row_ref[pl.ds(1, doms, stride=2), :]
    surface = jnp.dot(landing_ref[...], traces, preferred_element_type=F32)
    halves = []
    for p in range(NPAN):
        parts = []
        for t in range(3):
            pick = iota((16, LANE), 1) == iota((16, LANE), 0) + (48 * p + 16 * t)
            parts.append(turned(pick.astype(BF16), tails))
        halves.append((parts[2] + parts[1]) + parts[0])
    quads = jnp.concatenate(halves, axis=1)
    kernel_block = jnp.zeros_like(surface)
    for b in range(4):
        squared = jnp.zeros_like(surface)
        for c in range(3):
            shifted = spots_ref[:, c : c + 1] - quads[4 * c + b : 4 * c + b + 1, :]
            squared = squared + shifted * shifted
        green = jnp.cos(WAVE_NUMBER * jnp.sqrt(squared)) / (
            4.0 * math.pi * jnp.sqrt(squared + SMOOTHING * SMOOTHING)
        )
        kernel_block = kernel_block + quads[12 + b : 13 + b, :] * green
    panel_of(block_ref, panel_ref, doms)
    base_ref[...] = kernel_block - surface - placed(low_ref, panel_ref, core)


def far_kernel(block_ref, low_ref, base_ref, out_ref, panel_ref):
    core = lax.rem(lax.axis_index("col"), 2)
    panel_of(block_ref, panel_ref, block_ref.shape[0] // 18)
    out_ref[...] = base_ref[...] - placed(low_ref, panel_ref, 1 - core)


def near_stage(block, low, landing, spots):
    return pl.pallas_call(
        near_kernel,
        out_shape=jax.ShapeDtypeStruct((low.shape[0], LANE), F32),
        in_specs=[VM] * 4,
        out_specs=VM,
        scratch_shapes=[
            pltpu.VMEM(low.shape, BF16),
            pltpu.VMEM((2 * landing.shape[1], LANE), F32),
        ],
        compiler_params=PARAMS,
        cost_estimate=pl.CostEstimate(flops=40_000_000, bytes_accessed=1_000_000, transcendentals=100_000),
        name="near_stage",
    )(block, low, landing, spots)


def far_stage(block, low, base):
    return pl.pallas_call(
        far_kernel,
        out_shape=jax.ShapeDtypeStruct(base.shape, F32),
        in_specs=[VM] * 3,
        out_specs=VM,
        scratch_shapes=[pltpu.VMEM(low.shape, BF16)],
        compiler_params=PARAMS,
        name="far_stage",
    )(block, low, base)


def local(
    inverse,
    trace_map,
    panel_coupling,
    coupling,
    neighbours,
    iface_count,
    surface_rows,
    factor,
    colloc,
    quad_points,
    quad_weight,
    panel_block,
):
    doms = lax.axis_size("dom")
    cols = lax.axis_size("col")
    sent, inverse, trace_map, loads, factor_low, landing, spots = first_stage(
        inverse, trace_map, panel_coupling, coupling, neighbours, iface_count, surface_rows, factor,
        colloc, quad_points, quad_weight, doms,
    )
    got = lax.all_to_all(sent.reshape(doms, ROWS // 2, 2, LANE), "dom", 0, 0, tiled=True)
    sent, picks, lanes = mix_stage(got, panel_block, doms, cols)

    sent = sent.reshape(cols * doms, 2, LANE)
    correction = lax.all_to_all(sent, ("col", "dom"), 0, 0, tiled=True)
    correction = correction.reshape(cols, 2 * doms, LANE)
    pieces = second_stage(correction, loads, inverse, picks)
    gathered = lax.all_gather(pieces, "col", axis=0, tiled=False)

    sent = trace_stage(gathered, trace_map, lanes).reshape(doms, 9, 2, LANE)
    got = lax.all_to_all(sent, "dom", 0, 0, tiled=True)
    other = lax.ppermute(got, "col", [(c, c ^ 1) for c in range(cols)])
    base = near_stage(got.reshape(18 * doms, LANE), factor_low, landing, spots)
    return far_stage(other.reshape(18 * doms, LANE), factor_low, base)


def solution(mesh):
    in_specs = (
        P("dom", "col", None),
        P("dom", "col", None),
        P("dom", None, None),
        P("dom", None, "col"),
        P("dom", None),
        P(),
        P("dom", "col", None, None),
        P(("dom", "col"), None),
        P(None, ("dom", "col")),
        P(None, None, ("dom", "col")),
        P(None, ("dom", "col")),
        P(),
    )
    out_specs = P(("dom", "col"), None)
    return jax.shard_map(local, mesh=mesh, in_specs=in_specs, out_specs=out_specs, check_vma=False)
```

```python
import math

import jax
import jax.numpy as jnp
from jax import lax
from jax.experimental import pallas as pl
from jax.experimental.pallas import tpu as pltpu
from jax.sharding import PartitionSpec as P

MB = 208
P_SIZE = 64
NPAN = 2
LIVE = 128
MAX_LIVE = 112
LANE = 128
ROWS = 20

WAVE_NUMBER = 8.0
SMOOTHING = 0.05

F32 = jnp.float32
BF16 = jnp.bfloat16
VM = pl.BlockSpec(memory_space=pltpu.VMEM)
PARAMS = pltpu.CompilerParams(vmem_limit_bytes=16 * 1024 * 1024)


def iota(shape, axis):
    return lax.broadcasted_iota(jnp.int32, shape, axis)


def terms(values):
    high = values.astype(BF16).astype(F32)
    rest = values - high
    middle = rest.astype(BF16).astype(F32)
    return high, middle, rest - middle


def turned(left, right):
    return lax.dot_general(
        left, right.astype(BF16), (((1,), (1,)), ((), ())), preferred_element_type=F32
    )


def first_kernel(
    inv_hbm, loads_hbm, coup_hbm, listed_hbm, count_hbm, rows_hbm, factor_hbm, colloc_hbm,
    points_hbm, weight_hbm,
    sent_ref, inv_ref, loads_ref, low_ref, landing_ref, spots_ref,
    coup_in, listed_ref, count_ref, rows_ref, factor_ref, colloc_ref, points_ref, weight_ref,
    quad_ref, coup_scr, spot_scr, first_ref, row_ref, sems,
):
    doms = landing_ref.shape[1]
    moves = [
        pltpu.make_async_copy(src, dst, sems.at[i])
        for i, (src, dst) in enumerate(
            [
                (listed_hbm, listed_ref),
                (count_hbm, count_ref),
                (points_hbm, points_ref),
                (weight_hbm, weight_ref),
                (coup_hbm, coup_in),
                (rows_hbm, rows_ref),
                (colloc_hbm, colloc_ref),
                (loads_hbm, loads_ref),
                (inv_hbm.at[:, :LIVE], inv_ref),
                (factor_hbm, factor_ref),
            ]
        )
    ]
    for move in moves:
        move.start()
    coup_scr[...] = jnp.zeros_like(coup_scr)
    row_ref[...] = jnp.zeros_like(row_ref)
    spot_scr[...] = jnp.zeros_like(spot_scr)
    for move in moves[:7]:
        move.wait()
    count = count_ref[lax.axis_index("dom")]
    for c in range(3):
        quad_ref[4 * c : 4 * c + 4, :] = points_ref[c]
    quad_ref[12:16, :] = weight_ref[...]
    for k in range(6):
        coup_scr[k : k + 1, :] = coup_in[k][:, :LIVE]
    spot_scr[0:3, :] = colloc_ref[...]
    quads = jnp.concatenate(list(terms(quad_ref[...])) + [jnp.zeros((80, doms), F32)], axis=0)
    weights = list(terms(coup_scr[...]))
    even = jnp.concatenate([jnp.zeros((48, LIVE), F32)] + weights + [jnp.zeros((56, LIVE), F32)], axis=0)
    odd = jnp.concatenate([jnp.zeros((72, LIVE), F32)] + weights + [jnp.zeros((32, LIVE), F32)], axis=0)
    spots = jnp.concatenate(list(terms(spot_scr[...])) + [jnp.zeros((104, doms), F32)], axis=0)
    at = iota((doms, LIVE), 1)
    pair = 2 * iota((doms, LIVE), 0)
    unit = (iota((doms, doms), 0) == iota((doms, doms), 1)).astype(BF16)
    misc = turned(unit, quads)
    misc = misc + turned((at == pair).astype(BF16), even)
    misc = misc + turned((at == pair + 1).astype(BF16), odd)
    for k in range(6):
        misc = jnp.where(at == 96 + k, listed_ref[0, k].astype(F32), misc)
    misc = jnp.where(at == 102, count.astype(F32), misc)
    row_ref[pl.ds(2, doms, stride=4), :] = misc
    spots = turned(unit, spots)
    spots_ref[...] = spots + pltpu.roll(spots, LANE - 8, 1) + pltpu.roll(spots, LANE - 16, 1)
    landing_ref[...] = (iota((doms, doms), 0) == rows_ref[0, 0]).astype(BF16)
    for move in moves[7:9]:
        move.wait()
    first = jnp.dot(inv_ref[0], loads_ref[0], preferred_element_type=F32)
    first_ref[...] = jnp.where(iota((LIVE, LANE), 0) < count, first, 0.0)
    row_ref[pl.ds(0, doms, stride=4), :] = first_ref[pl.ds(0, doms, stride=2), :]
    row_ref[pl.ds(1, doms, stride=4), :] = first_ref[pl.ds(1, doms, stride=2), :]
    for h in range(doms):
        sent_ref[ROWS * h + 16 : ROWS * h + 20, :] = row_ref[4 * h : 4 * h + 4, :].astype(BF16)
    moves[9].wait()
    for h in range(doms):
        tile = factor_ref[pl.ds(16 * (h // 16), 16), pl.ds(LANE * (h % 16), LANE)]
        sent_ref[ROWS * h : ROWS * h + 16, :] = tile.astype(BF16)
    low_ref[...] = factor_ref[...].astype(BF16)


def first_stage(
    inverse, panel_coupling, coupling, neighbours, iface_count, surface_rows, factor,
    colloc, quad_points, quad_weight, doms,
):
    shape = jax.ShapeDtypeStruct
    coupling = coupling.transpose(1, 0, 2)
    return pl.pallas_call(
        first_kernel,
        out_shape=(
            shape((ROWS * doms, LANE), BF16),
            shape((1, LIVE, inverse.shape[2]), BF16),
            shape(panel_coupling.shape, BF16),
            shape(factor.shape, BF16),
            shape((doms, doms), BF16),
            shape((doms, LANE), F32),
        ),
        in_specs=[pl.BlockSpec(memory_space=pltpu.HBM)] * 10,
        out_specs=(VM,) * 6,
        scratch_shapes=[
            pltpu.VMEM(coupling.shape, F32),
            pltpu.SMEM(neighbours.shape, jnp.int32),
            pltpu.SMEM(iface_count.shape, jnp.int32),
            pltpu.VMEM(surface_rows.shape, jnp.int32),
            pltpu.VMEM(factor.shape, F32),
            pltpu.VMEM(colloc.shape, F32),
            pltpu.VMEM(quad_points.shape, F32),
            pltpu.VMEM(quad_weight.shape, F32),
            pltpu.VMEM((16, doms), F32),
            pltpu.VMEM((8, LIVE), F32),
            pltpu.VMEM((8, doms), F32),
            pltpu.VMEM((LIVE, LANE), F32),
            pltpu.VMEM((4 * doms, LANE), F32),
            pltpu.SemaphoreType.DMA((10,)),
        ],
        compiler_params=PARAMS,
        name="first_stage",
    )(
        *(
            pltpu.with_memory_space_constraint(x, pltpu.HBM)
            for x in (
                inverse, panel_coupling, coupling, neighbours, iface_count, surface_rows,
                factor, colloc, quad_points, quad_weight,
            )
        )
    )


def mix_kernel(
    got_ref, pair_ref, block_hbm, inv_hbm, map_hbm, sent_ref, picks_ref, lane_ref, rest_ref, map_ref, block_ref, row_ref, sem
):
    doms = pair_ref.shape[0]
    cols = sent_ref.shape[0]
    move = pltpu.make_async_copy(block_hbm, block_ref, sem.at[0])
    move.start()
    rest = pltpu.make_async_copy(inv_hbm.at[:, LIVE:], rest_ref, sem.at[1])
    rest.start()
    maps = pltpu.make_async_copy(map_hbm, map_ref, sem.at[2])
    maps.start()
    for h in range(doms):
        row_ref[4 * h : 4 * h + 4, :] = got_ref[ROWS * h + 16 : ROWS * h + 20, :].astype(F32)
    misc = row_ref[pl.ds(2, doms, stride=4), :]
    weights = misc + pltpu.roll(misc, LANE - 8, 1) + pltpu.roll(misc, LANE - 16, 1)
    sources = iota((doms, doms), 1).astype(F32)
    mixed = []
    for r in range(2):
        mixing = jnp.zeros((doms, doms), F32)
        for k in range(6):
            lane = 48 + 24 * r + k
            mixing = mixing + jnp.where(
                misc[:, 96 + k : 97 + k] == sources, weights[:, lane : lane + 1], 0.0
            )
        summed = jnp.dot(
            mixing,
            row_ref[pl.ds(r, doms, stride=4), :],
            precision=lax.Precision.HIGHEST,
            preferred_element_type=F32,
        )
        row = (2 * lax.axis_index("dom") + r).astype(F32)
        mixed.append(jnp.where(misc[:, 102:103] > row, summed, 0.0))
    row_ref[pl.ds(0, doms, stride=2), :] = mixed[0]
    row_ref[pl.ds(1, doms, stride=2), :] = mixed[1]
    correction = row_ref[: 2 * doms, :].astype(BF16)
    for c in range(cols):
        sent_ref[c] = correction
    move.wait()
    for p in range(NPAN):
        owner = lax.div(block_ref[p], cols)
        picks_ref[p] = pair_ref[pl.ds(owner, 1)][0]
        lane_ref[p] = jnp.full((8, LANE), lax.rem(block_ref[p], cols), jnp.int32)
    rest.wait()
    maps.wait()


def mix_stage(got, panel_block, inverse, trace_map, doms, cols):
    return pl.pallas_call(
        mix_kernel,
        out_shape=(
            jax.ShapeDtypeStruct((cols, 2 * doms, LANE), BF16),
            jax.ShapeDtypeStruct((NPAN, ROWS // 2, 2, LANE), BF16),
            jax.ShapeDtypeStruct((NPAN, 8, LANE), jnp.int32),
            jax.ShapeDtypeStruct((1, MB - LIVE, inverse.shape[2]), BF16),
            jax.ShapeDtypeStruct(trace_map.shape, BF16),
        ),
        in_specs=[VM, VM] + [pl.BlockSpec(memory_space=pltpu.HBM)] * 3,
        out_specs=(VM,) * 5,
        scratch_shapes=[
            pltpu.SMEM(panel_block.shape, jnp.int32),
            pltpu.VMEM((4 * doms, LANE), F32),
            pltpu.SemaphoreType.DMA((3,)),
        ],
        compiler_params=PARAMS,
        name="mix_stage",
    )(
        got.reshape(ROWS * doms, LANE),
        got,
        pltpu.with_memory_space_constraint(panel_block, pltpu.HBM),
        pltpu.with_memory_space_constraint(inverse, pltpu.HBM),
        pltpu.with_memory_space_constraint(trace_map, pltpu.HBM),
    )


def second_kernel(correction_ref, loads_ref, inv_ref, rest_ref, picks_ref, out_ref, loaded_ref):
    cols = correction_ref.shape[0]
    for c in range(cols):
        top = loads_ref[0, MB * c : MB * c + MAX_LIVE, :].astype(F32)
        top = top - correction_ref[c, :MAX_LIVE, :].astype(F32)
        loaded_ref[MB * c : MB * c + MAX_LIVE, :] = top.astype(BF16)
        loaded_ref[MB * c + MAX_LIVE : MB * (c + 1), :] = loads_ref[0, MB * c + MAX_LIVE : MB * (c + 1), :]
    top = jnp.dot(inv_ref[0], loaded_ref[...], preferred_element_type=F32)
    out_ref[:LIVE, :] = top.astype(BF16)
    bottom = jnp.dot(rest_ref[0], loaded_ref[...], preferred_element_type=F32)
    out_ref[LIVE:MB, :] = bottom.astype(BF16)
    out_ref[MB + 32 :, :] = jnp.zeros((16, LANE), BF16)
    for p in range(NPAN):
        out_ref[MB + 16 * p : MB + 16 * p + 16, :] = picks_ref[ROWS * p : ROWS * p + 16, :]
        out_ref[MB + 32 + 2 * p : MB + 34 + 2 * p, :] = picks_ref[ROWS * p + 18 : ROWS * p + 20, :]


def second_stage(correction, loads, inverse, rest, picks):
    return pl.pallas_call(
        second_kernel,
        out_shape=jax.ShapeDtypeStruct((MB + 48, LANE), BF16),
        in_specs=[VM] * 5,
        out_specs=VM,
        scratch_shapes=[pltpu.VMEM(loads.shape[1:], BF16)],
        compiler_params=PARAMS,
        name="second_stage",
    )(correction, loads, inverse, rest, picks.reshape(NPAN * ROWS, LANE))


def trace_kernel(gathered_ref, map_ref, lane_ref, sent_ref, second_ref, row_ref):
    cols = gathered_ref.shape[0]
    doms = map_ref.shape[1]
    first_core = lax.rem(lax.axis_index("col"), 2) == 0
    lanes = [lane_ref[p][:1, :] for p in range(NPAN)]
    chunk = jnp.zeros((16, LANE), F32)
    quads = [jnp.zeros((1, LANE), F32)] * NPAN
    for c in range(cols):
        second_ref[MB * c : MB * (c + 1), :] = gathered_ref[c, :MB, :]
        rest = gathered_ref[c, MB : MB + 48, :].astype(F32)
        tile = jnp.where(first_core, rest[:16], rest[16:32])
        chunk = jnp.where(jnp.where(first_core, lanes[0], lanes[1]) == c, tile, chunk)
        for p in range(NPAN):
            quads[p] = jnp.where(lanes[p] == c, rest[32 + 2 * p : 33 + 2 * p], quads[p])
    tail = jnp.where(iota((1, LANE), 1) < 48, quads[0], pltpu.roll(quads[1], 48, 1))
    row_ref[pl.ds(1, doms, stride=2), :] = jnp.broadcast_to(tail, (doms, LANE))
    row_ref[pl.ds(0, doms, stride=2), :] = jnp.dot(
        map_ref[0], second_ref[...], preferred_element_type=F32
    )
    chunk = chunk.astype(BF16)
    for h in range(doms):
        sent_ref[18 * h : 18 * h + 16, :] = chunk
        sent_ref[18 * h + 16 : 18 * h + 18, :] = row_ref[2 * h : 2 * h + 2, :].astype(BF16)


def trace_stage(gathered, trace_map, lanes):
    doms = trace_map.shape[1]
    return pl.pallas_call(
        trace_kernel,
        out_shape=jax.ShapeDtypeStruct((18 * doms, LANE), BF16),
        in_specs=[VM, VM, VM],
        out_specs=VM,
        scratch_shapes=[
            pltpu.VMEM((trace_map.shape[2], LANE), BF16),
            pltpu.VMEM((2 * doms, LANE), F32),
        ],
        compiler_params=PARAMS,
        name="trace_stage",
    )(gathered, trace_map, lanes)


def panel_of(block_ref, panel_ref, doms):
    for h in range(doms):
        tile = block_ref[18 * h : 18 * h + 16, :]
        panel_ref[pl.ds(16 * (h // 16), 16), pl.ds(LANE * (h % 16), LANE)] = tile


def placed(low_ref, panel_ref, side):
    prior = lax.dot_general(
        low_ref[...], panel_ref[...], (((1,), (1,)), ((), ())), preferred_element_type=F32
    )
    both = jnp.concatenate([prior, prior], axis=1)
    return jnp.where((iota(both.shape, 1) >= P_SIZE) == (side == 1), both, 0.0)


def near_kernel(block_ref, low_ref, landing_ref, spots_ref, base_ref, panel_ref, row_ref):
    doms = landing_ref.shape[1]
    core = lax.rem(lax.axis_index("col"), 2)
    for h in range(doms):
        row_ref[2 * h : 2 * h + 2, :] = block_ref[18 * h + 16 : 18 * h + 18, :].astype(F32)
    traces = row_ref[pl.ds(0, doms, stride=2), :].astype(BF16)
    tails = row_ref[pl.ds(1, doms, stride=2), :]
    surface = jnp.dot(landing_ref[...], traces, preferred_element_type=F32)
    halves = []
    for p in range(NPAN):
        parts = []
        for t in range(3):
            pick = iota((16, LANE), 1) == iota((16, LANE), 0) + (48 * p + 16 * t)
            parts.append(turned(pick.astype(BF16), tails))
        halves.append((parts[2] + parts[1]) + parts[0])
    quads = jnp.concatenate(halves, axis=1)
    kernel_block = jnp.zeros_like(surface)
    for b in range(4):
        squared = jnp.zeros_like(surface)
        for c in range(3):
            shifted = spots_ref[:, c : c + 1] - quads[4 * c + b : 4 * c + b + 1, :]
            squared = squared + shifted * shifted
        green = jnp.cos(WAVE_NUMBER * jnp.sqrt(squared)) / (
            4.0 * math.pi * jnp.sqrt(squared + SMOOTHING * SMOOTHING)
        )
        kernel_block = kernel_block + quads[12 + b : 13 + b, :] * green
    panel_of(block_ref, panel_ref, doms)
    base_ref[...] = kernel_block - surface - placed(low_ref, panel_ref, core)


def far_kernel(block_ref, low_ref, base_ref, out_ref, panel_ref):
    core = lax.rem(lax.axis_index("col"), 2)
    panel_of(block_ref, panel_ref, block_ref.shape[0] // 18)
    out_ref[...] = base_ref[...] - placed(low_ref, panel_ref, 1 - core)


def near_stage(block, low, landing, spots):
    return pl.pallas_call(
        near_kernel,
        out_shape=jax.ShapeDtypeStruct((low.shape[0], LANE), F32),
        in_specs=[VM] * 4,
        out_specs=VM,
        scratch_shapes=[
            pltpu.VMEM(low.shape, BF16),
            pltpu.VMEM((2 * landing.shape[1], LANE), F32),
        ],
        compiler_params=PARAMS,
        cost_estimate=pl.CostEstimate(flops=40_000_000, bytes_accessed=1_000_000, transcendentals=100_000),
        name="near_stage",
    )(block, low, landing, spots)


def far_stage(block, low, base):
    return pl.pallas_call(
        far_kernel,
        out_shape=jax.ShapeDtypeStruct(base.shape, F32),
        in_specs=[VM] * 3,
        out_specs=VM,
        scratch_shapes=[pltpu.VMEM(low.shape, BF16)],
        compiler_params=PARAMS,
        name="far_stage",
    )(block, low, base)


def local(
    inverse,
    trace_map,
    panel_coupling,
    coupling,
    neighbours,
    iface_count,
    surface_rows,
    factor,
    colloc,
    quad_points,
    quad_weight,
    panel_block,
):
    doms = lax.axis_size("dom")
    cols = lax.axis_size("col")
    sent, top, loads, factor_low, landing, spots = first_stage(
        inverse, panel_coupling, coupling, neighbours, iface_count, surface_rows, factor,
        colloc, quad_points, quad_weight, doms,
    )
    got = lax.all_to_all(sent.reshape(doms, ROWS // 2, 2, LANE), "dom", 0, 0, tiled=True)
    sent, picks, lanes, rest, trace_map = mix_stage(
        got, panel_block, inverse, trace_map, doms, cols
    )

    sent = sent.reshape(cols * doms, 2, LANE)
    correction = lax.all_to_all(sent, ("col", "dom"), 0, 0, tiled=True)
    correction = correction.reshape(cols, 2 * doms, LANE)
    pieces = second_stage(correction, loads, top, rest, picks)
    gathered = lax.all_gather(pieces, "col", axis=0, tiled=False)

    sent = trace_stage(gathered, trace_map, lanes).reshape(doms, 9, 2, LANE)
    got = lax.all_to_all(sent, "dom", 0, 0, tiled=True)
    other = lax.ppermute(got, "col", [(c, c ^ 1) for c in range(cols)])
    base = near_stage(got.reshape(18 * doms, LANE), factor_low, landing, spots)
    return far_stage(other.reshape(18 * doms, LANE), factor_low, base)


def solution(mesh):
    in_specs = (
        P("dom", "col", None),
        P("dom", "col", None),
        P("dom", None, None),
        P("dom", None, "col"),
        P("dom", None),
        P(),
        P("dom", "col", None, None),
        P(("dom", "col"), None),
        P(None, ("dom", "col")),
        P(None, None, ("dom", "col")),
        P(None, ("dom", "col")),
        P(),
    )
    out_specs = P(("dom", "col"), None)
    return jax.shard_map(local, mesh=mesh, in_specs=in_specs, out_specs=out_specs, check_vma=False)
```

```python
import math

import jax
import jax.numpy as jnp
from jax import lax
from jax.experimental import pallas as pl
from jax.experimental.pallas import tpu as pltpu
from jax.sharding import PartitionSpec as P

MB = 208
P_SIZE = 64
NPAN = 2
LIVE = 128
MAX_LIVE = 112
LANE = 128
ROWS = 20

WAVE_NUMBER = 8.0
SMOOTHING = 0.05

F32 = jnp.float32
BF16 = jnp.bfloat16
VM = pl.BlockSpec(memory_space=pltpu.VMEM)
PARAMS = pltpu.CompilerParams(vmem_limit_bytes=16 * 1024 * 1024)


def iota(shape, axis):
    return lax.broadcasted_iota(jnp.int32, shape, axis)


def terms(values):
    high = values.astype(BF16).astype(F32)
    rest = values - high
    middle = rest.astype(BF16).astype(F32)
    return high, middle, rest - middle


def turned(left, right):
    return lax.dot_general(
        left, right.astype(BF16), (((1,), (1,)), ((), ())), preferred_element_type=F32
    )


def first_kernel(
    inv_hbm, map_hbm, loads_hbm, coup_hbm, listed_hbm, count_hbm, rows_hbm, factor_hbm, colloc_hbm,
    points_hbm, weight_hbm,
    sent_ref, inv_ref, map_ref, loads_ref, low_ref, landing_ref, spots_ref,
    coup_in, listed_ref, count_ref, rows_ref, factor_ref, colloc_ref, points_ref, weight_ref,
    quad_ref, coup_scr, spot_scr, first_ref, row_ref, sems,
):
    doms = landing_ref.shape[1]
    moves = [
        pltpu.make_async_copy(src, dst, sems.at[i])
        for i, (src, dst) in enumerate(
            [
                (listed_hbm, listed_ref),
                (count_hbm, count_ref),
                (points_hbm, points_ref),
                (weight_hbm, weight_ref),
                (coup_hbm, coup_in),
                (rows_hbm, rows_ref),
                (colloc_hbm, colloc_ref),
                (loads_hbm, loads_ref),
                (inv_hbm.at[:, :LIVE], inv_ref.at[:, :LIVE]),
                (factor_hbm, factor_ref),
                (inv_hbm.at[:, LIVE:], inv_ref.at[:, LIVE:]),
                (map_hbm, map_ref),
            ]
        )
    ]
    for move in moves:
        move.start()
    coup_scr[...] = jnp.zeros_like(coup_scr)
    row_ref[...] = jnp.zeros_like(row_ref)
    spot_scr[...] = jnp.zeros_like(spot_scr)
    for move in moves[:7]:
        move.wait()
    count = count_ref[lax.axis_index("dom")]
    for c in range(3):
        quad_ref[4 * c : 4 * c + 4, :] = points_ref[c]
    quad_ref[12:16, :] = weight_ref[...]
    for k in range(6):
        coup_scr[k : k + 1, :] = coup_in[k][:, :LIVE]
    spot_scr[0:3, :] = colloc_ref[...]
    quads = jnp.concatenate(list(terms(quad_ref[...])) + [jnp.zeros((80, doms), F32)], axis=0)
    weights = list(terms(coup_scr[...]))
    even = jnp.concatenate([jnp.zeros((48, LIVE), F32)] + weights + [jnp.zeros((56, LIVE), F32)], axis=0)
    odd = jnp.concatenate([jnp.zeros((72, LIVE), F32)] + weights + [jnp.zeros((32, LIVE), F32)], axis=0)
    spots = jnp.concatenate(list(terms(spot_scr[...])) + [jnp.zeros((104, doms), F32)], axis=0)
    at = iota((doms, LIVE), 1)
    pair = 2 * iota((doms, LIVE), 0)
    unit = (iota((doms, doms), 0) == iota((doms, doms), 1)).astype(BF16)
    misc = turned(unit, quads)
    misc = misc + turned((at == pair).astype(BF16), even)
    misc = misc + turned((at == pair + 1).astype(BF16), odd)
    for k in range(6):
        misc = jnp.where(at == 96 + k, listed_ref[0, k].astype(F32), misc)
    misc = jnp.where(at == 102, count.astype(F32), misc)
    row_ref[pl.ds(2, doms, stride=4), :] = misc
    spots = turned(unit, spots)
    spots_ref[...] = spots + pltpu.roll(spots, LANE - 8, 1) + pltpu.roll(spots, LANE - 16, 1)
    landing_ref[...] = (iota((doms, doms), 0) == rows_ref[0, 0]).astype(BF16)
    for move in moves[7:9]:
        move.wait()
    first = jnp.dot(inv_ref[0, :LIVE, :], loads_ref[0], preferred_element_type=F32)
    first_ref[...] = jnp.where(iota((LIVE, LANE), 0) < count, first, 0.0)
    row_ref[pl.ds(0, doms, stride=4), :] = first_ref[pl.ds(0, doms, stride=2), :]
    row_ref[pl.ds(1, doms, stride=4), :] = first_ref[pl.ds(1, doms, stride=2), :]
    for h in range(doms):
        sent_ref[ROWS * h + 16 : ROWS * h + 20, :] = row_ref[4 * h : 4 * h + 4, :].astype(BF16)
    moves[9].wait()
    for h in range(doms):
        tile = factor_ref[pl.ds(16 * (h // 16), 16), pl.ds(LANE * (h % 16), LANE)]
        sent_ref[ROWS * h : ROWS * h + 16, :] = tile.astype(BF16)
    low_ref[...] = factor_ref[...].astype(BF16)
    for move in moves[10:]:
        move.wait()


def first_stage(
    inverse, trace_map, panel_coupling, coupling, neighbours, iface_count, surface_rows, factor,
    colloc, quad_points, quad_weight, doms,
):
    shape = jax.ShapeDtypeStruct
    coupling = coupling.transpose(1, 0, 2)
    return pl.pallas_call(
        first_kernel,
        out_shape=(
            shape((ROWS * doms, LANE), BF16),
            shape(inverse.shape, BF16),
            shape(trace_map.shape, BF16),
            shape(panel_coupling.shape, BF16),
            shape(factor.shape, BF16),
            shape((doms, doms), BF16),
            shape((doms, LANE), F32),
        ),
        in_specs=[pl.BlockSpec(memory_space=pltpu.HBM)] * 11,
        out_specs=(VM,) * 7,
        scratch_shapes=[
            pltpu.VMEM(coupling.shape, F32),
            pltpu.SMEM(neighbours.shape, jnp.int32),
            pltpu.SMEM(iface_count.shape, jnp.int32),
            pltpu.VMEM(surface_rows.shape, jnp.int32),
            pltpu.VMEM(factor.shape, F32),
            pltpu.VMEM(colloc.shape, F32),
            pltpu.VMEM(quad_points.shape, F32),
            pltpu.VMEM(quad_weight.shape, F32),
            pltpu.VMEM((16, doms), F32),
            pltpu.VMEM((8, LIVE), F32),
            pltpu.VMEM((8, doms), F32),
            pltpu.VMEM((LIVE, LANE), F32),
            pltpu.VMEM((4 * doms, LANE), F32),
            pltpu.SemaphoreType.DMA((12,)),
        ],
        compiler_params=PARAMS,
        name="first_stage",
    )(
        *(
            pltpu.with_memory_space_constraint(x, pltpu.HBM)
            for x in (
                inverse, trace_map, panel_coupling, coupling, neighbours, iface_count, surface_rows,
                factor, colloc, quad_points, quad_weight,
            )
        )
    )


def mix_kernel(got_ref, pair_ref, block_hbm, sent_ref, picks_ref, lane_ref, block_ref, row_ref, sem):
    doms = pair_ref.shape[0]
    cols = sent_ref.shape[0]
    move = pltpu.make_async_copy(block_hbm, block_ref, sem.at[0])
    move.start()
    for h in range(doms):
        row_ref[4 * h : 4 * h + 4, :] = got_ref[ROWS * h + 16 : ROWS * h + 20, :].astype(F32)
    misc = row_ref[pl.ds(2, doms, stride=4), :]
    weights = misc + pltpu.roll(misc, LANE - 8, 1) + pltpu.roll(misc, LANE - 16, 1)
    sources = iota((doms, doms), 1).astype(F32)
    mixed = []
    for r in range(2):
        mixing = jnp.zeros((doms, doms), F32)
        for k in range(6):
            lane = 48 + 24 * r + k
            mixing = mixing + jnp.where(
                misc[:, 96 + k : 97 + k] == sources, weights[:, lane : lane + 1], 0.0
            )
        values = row_ref[pl.ds(r, doms, stride=4), :].astype(BF16)
        summed = jnp.zeros((doms, LANE), F32)
        for term in reversed(terms(mixing)):
            summed = summed + jnp.dot(term.astype(BF16), values, preferred_element_type=F32)
        row = (2 * lax.axis_index("dom") + r).astype(F32)
        mixed.append(jnp.where(misc[:, 102:103] > row, summed, 0.0))
    row_ref[pl.ds(0, doms, stride=2), :] = mixed[0]
    row_ref[pl.ds(1, doms, stride=2), :] = mixed[1]
    correction = row_ref[: 2 * doms, :].astype(BF16)
    for c in range(cols):
        sent_ref[c] = correction
    move.wait()
    for p in range(NPAN):
        owner = lax.div(block_ref[p], cols)
        picks_ref[p] = pair_ref[pl.ds(owner, 1)][0]
        lane_ref[p] = jnp.full((8, LANE), lax.rem(block_ref[p], cols), jnp.int32)


def mix_stage(got, panel_block, doms, cols):
    return pl.pallas_call(
        mix_kernel,
        out_shape=(
            jax.ShapeDtypeStruct((cols, 2 * doms, LANE), BF16),
            jax.ShapeDtypeStruct((NPAN, ROWS // 2, 2, LANE), BF16),
            jax.ShapeDtypeStruct((NPAN, 8, LANE), jnp.int32),
        ),
        in_specs=[VM, VM, pl.BlockSpec(memory_space=pltpu.HBM)],
        out_specs=(VM, VM, VM),
        scratch_shapes=[
            pltpu.SMEM(panel_block.shape, jnp.int32),
            pltpu.VMEM((4 * doms, LANE), F32),
            pltpu.SemaphoreType.DMA((1,)),
        ],
        compiler_params=PARAMS,
        name="mix_stage",
    )(
        got.reshape(ROWS * doms, LANE),
        got,
        pltpu.with_memory_space_constraint(panel_block, pltpu.HBM),
    )


def second_kernel(correction_ref, loads_ref, inv_ref, picks_ref, out_ref, loaded_ref):
    cols = correction_ref.shape[0]
    for c in range(cols):
        top = loads_ref[0, MB * c : MB * c + MAX_LIVE, :].astype(F32)
        top = top - correction_ref[c, :MAX_LIVE, :].astype(F32)
        loaded_ref[MB * c : MB * c + MAX_LIVE, :] = top.astype(BF16)
        loaded_ref[MB * c + MAX_LIVE : MB * (c + 1), :] = loads_ref[0, MB * c + MAX_LIVE : MB * (c + 1), :]
    second = jnp.dot(inv_ref[0], loaded_ref[...], preferred_element_type=F32)
    out_ref[:MB, :] = second.astype(BF16)
    out_ref[MB + 32 :, :] = jnp.zeros((16, LANE), BF16)
    for p in range(NPAN):
        out_ref[MB + 16 * p : MB + 16 * p + 16, :] = picks_ref[ROWS * p : ROWS * p + 16, :]
        out_ref[MB + 32 + 2 * p : MB + 34 + 2 * p, :] = picks_ref[ROWS * p + 18 : ROWS * p + 20, :]


def second_stage(correction, loads, inverse, picks):
    return pl.pallas_call(
        second_kernel,
        out_shape=jax.ShapeDtypeStruct((MB + 48, LANE), BF16),
        in_specs=[VM] * 4,
        out_specs=VM,
        scratch_shapes=[pltpu.VMEM(loads.shape[1:], BF16)],
        compiler_params=PARAMS,
        name="second_stage",
    )(correction, loads, inverse, picks.reshape(NPAN * ROWS, LANE))


def trace_kernel(gathered_ref, map_ref, lane_ref, sent_ref, second_ref, row_ref):
    cols = gathered_ref.shape[0]
    doms = map_ref.shape[1]
    first_core = lax.rem(lax.axis_index("col"), 2) == 0
    lanes = [lane_ref[p][:1, :] for p in range(NPAN)]
    chunk = jnp.zeros((16, LANE), F32)
    quads = [jnp.zeros((1, LANE), F32)] * NPAN
    for c in range(cols):
        second_ref[MB * c : MB * (c + 1), :] = gathered_ref[c, :MB, :]
        rest = gathered_ref[c, MB : MB + 48, :].astype(F32)
        tile = jnp.where(first_core, rest[:16], rest[16:32])
        chunk = jnp.where(jnp.where(first_core, lanes[0], lanes[1]) == c, tile, chunk)
        for p in range(NPAN):
            quads[p] = jnp.where(lanes[p] == c, rest[32 + 2 * p : 33 + 2 * p], quads[p])
    tail = jnp.where(iota((1, LANE), 1) < 48, quads[0], pltpu.roll(quads[1], 48, 1))
    row_ref[pl.ds(1, doms, stride=2), :] = jnp.broadcast_to(tail, (doms, LANE))
    row_ref[pl.ds(0, doms, stride=2), :] = jnp.dot(
        map_ref[0], second_ref[...], preferred_element_type=F32
    )
    chunk = chunk.astype(BF16)
    for h in range(doms):
        sent_ref[18 * h : 18 * h + 16, :] = chunk
        sent_ref[18 * h + 16 : 18 * h + 18, :] = row_ref[2 * h : 2 * h + 2, :].astype(BF16)


def trace_stage(gathered, trace_map, lanes):
    doms = trace_map.shape[1]
    return pl.pallas_call(
        trace_kernel,
        out_shape=jax.ShapeDtypeStruct((18 * doms, LANE), BF16),
        in_specs=[VM, VM, VM],
        out_specs=VM,
        scratch_shapes=[
            pltpu.VMEM((trace_map.shape[2], LANE), BF16),
            pltpu.VMEM((2 * doms, LANE), F32),
        ],
        compiler_params=PARAMS,
        name="trace_stage",
    )(gathered, trace_map, lanes)


def panel_of(block_ref, panel_ref, doms):
    for h in range(doms):
        tile = block_ref[18 * h : 18 * h + 16, :]
        panel_ref[pl.ds(16 * (h // 16), 16), pl.ds(LANE * (h % 16), LANE)] = tile


def placed(low_ref, panel_ref, side):
    prior = lax.dot_general(
        low_ref[...], panel_ref[...], (((1,), (1,)), ((), ())), preferred_element_type=F32
    )
    both = jnp.concatenate([prior, prior], axis=1)
    return jnp.where((iota(both.shape, 1) >= P_SIZE) == (side == 1), both, 0.0)


def near_kernel(block_ref, low_ref, landing_ref, spots_ref, base_ref, panel_ref, row_ref):
    doms = landing_ref.shape[1]
    core = lax.rem(lax.axis_index("col"), 2)
    for h in range(doms):
        row_ref[2 * h : 2 * h + 2, :] = block_ref[18 * h + 16 : 18 * h + 18, :].astype(F32)
    traces = row_ref[pl.ds(0, doms, stride=2), :].astype(BF16)
    tails = row_ref[pl.ds(1, doms, stride=2), :]
    surface = jnp.dot(landing_ref[...], traces, preferred_element_type=F32)
    halves = []
    for p in range(NPAN):
        parts = []
        for t in range(3):
            pick = iota((16, LANE), 1) == iota((16, LANE), 0) + (48 * p + 16 * t)
            parts.append(turned(pick.astype(BF16), tails))
        halves.append((parts[2] + parts[1]) + parts[0])
    quads = jnp.concatenate(halves, axis=1)
    kernel_block = jnp.zeros_like(surface)
    for b in range(4):
        squared = jnp.zeros_like(surface)
        for c in range(3):
            shifted = spots_ref[:, c : c + 1] - quads[4 * c + b : 4 * c + b + 1, :]
            squared = squared + shifted * shifted
        green = jnp.cos(WAVE_NUMBER * jnp.sqrt(squared)) / (
            4.0 * math.pi * jnp.sqrt(squared + SMOOTHING * SMOOTHING)
        )
        kernel_block = kernel_block + quads[12 + b : 13 + b, :] * green
    panel_of(block_ref, panel_ref, doms)
    base_ref[...] = kernel_block - surface - placed(low_ref, panel_ref, core)


def far_kernel(block_ref, low_ref, base_ref, out_ref, panel_ref):
    core = lax.rem(lax.axis_index("col"), 2)
    panel_of(block_ref, panel_ref, block_ref.shape[0] // 18)
    out_ref[...] = base_ref[...] - placed(low_ref, panel_ref, 1 - core)


def near_stage(block, low, landing, spots):
    return pl.pallas_call(
        near_kernel,
        out_shape=jax.ShapeDtypeStruct((low.shape[0], LANE), F32),
        in_specs=[VM] * 4,
        out_specs=VM,
        scratch_shapes=[
            pltpu.VMEM(low.shape, BF16),
            pltpu.VMEM((2 * landing.shape[1], LANE), F32),
        ],
        compiler_params=PARAMS,
        cost_estimate=pl.CostEstimate(flops=40_000_000, bytes_accessed=1_000_000, transcendentals=100_000),
        name="near_stage",
    )(block, low, landing, spots)


def far_stage(block, low, base):
    return pl.pallas_call(
        far_kernel,
        out_shape=jax.ShapeDtypeStruct(base.shape, F32),
        in_specs=[VM] * 3,
        out_specs=VM,
        scratch_shapes=[pltpu.VMEM(low.shape, BF16)],
        compiler_params=PARAMS,
        name="far_stage",
    )(block, low, base)


def local(
    inverse,
    trace_map,
    panel_coupling,
    coupling,
    neighbours,
    iface_count,
    surface_rows,
    factor,
    colloc,
    quad_points,
    quad_weight,
    panel_block,
):
    doms = lax.axis_size("dom")
    cols = lax.axis_size("col")
    sent, inverse, trace_map, loads, factor_low, landing, spots = first_stage(
        inverse, trace_map, panel_coupling, coupling, neighbours, iface_count, surface_rows, factor,
        colloc, quad_points, quad_weight, doms,
    )
    got = lax.all_to_all(sent.reshape(doms, ROWS // 2, 2, LANE), "dom", 0, 0, tiled=True)
    sent, picks, lanes = mix_stage(got, panel_block, doms, cols)

    sent = sent.reshape(cols * doms, 2, LANE)
    correction = lax.all_to_all(sent, ("col", "dom"), 0, 0, tiled=True)
    correction = correction.reshape(cols, 2 * doms, LANE)
    pieces = second_stage(correction, loads, inverse, picks)
    gathered = lax.all_gather(pieces, "col", axis=0, tiled=False)

    sent = trace_stage(gathered, trace_map, lanes).reshape(doms, 9, 2, LANE)
    got = lax.all_to_all(sent, "dom", 0, 0, tiled=True)
    other = lax.ppermute(got, "col", [(c, c ^ 1) for c in range(cols)])
    base = near_stage(got.reshape(18 * doms, LANE), factor_low, landing, spots)
    return far_stage(other.reshape(18 * doms, LANE), factor_low, base)


def solution(mesh):
    in_specs = (
        P("dom", "col", None),
        P("dom", "col", None),
        P("dom", None, None),
        P("dom", None, "col"),
        P("dom", None),
        P(),
        P("dom", "col", None, None),
        P(("dom", "col"), None),
        P(None, ("dom", "col")),
        P(None, None, ("dom", "col")),
        P(None, ("dom", "col")),
        P(),
    )
    out_specs = P(("dom", "col"), None)
    return jax.shard_map(local, mesh=mesh, in_specs=in_specs, out_specs=out_specs, check_vma=False)
```
